512 devices in a mesh: sub: 4 (over z_lo), row: 16 (over z_hi, x, core), col: 8 (over y).
Axes of the slice: x: 4, y: 8, z: 8 (z_hi: 2, z_lo: 4; z = z_hi * 4 + z_lo), core: 2. Of those that a mesh axis runs over, the one named last changes fastest.
Arguments:
- child_update: bfloat16 [32768, 8192], P(('sub', 'row'), 'col'), may hold values from -2.8 to 2.8, as said below
- parent_front: bfloat16 [16384, 16384], P('row', ('sub', 'col')), may hold values from -2.8 to 256, as said below
- tile_map: int32 [4, 64], replicated, may hold values from -1 to 127, as said below
Outputs:
- front_out: float32 [16384, 16384], P('row', ('sub', 'col'))
The draws below stay inside these ranges and needn't reach their ends.
Inputs may be any that keep to these rules, and one draw needn't show every extreme that they name: Live tiles of a child come first, a whole multiple of 16 of them, at least max(1, 2) * 16; then -1. At least one child has all 64 tiles live. Within one child the parent tiles are distinct, and (tile_map[s, j] // 4) % 16 == j % 16 for every live j. `child_update`: each child's update, in logical order, is a symmetric matrix. `parent_front`: symmetric in logical order, with diagonal entries between 64 and 256; the assembled leading 4 x 4 tiles are positive definite.
All inputs are finite; a program needn't handle non-finite values.
Results may differ from the reference program's by a relative error of at most 0.0008.
Values may be sent and summed in bfloat16 or wider, within the bound.
A program may use at most 64 MiB of HBM per device.

```python
import jax
import jax.numpy as jnp
from jax import lax

TILE = 128
PANEL = 4
CRL = 4
CT = 64
CCL = 8
PT = 128
PRL = 8
N_SUB = 4
N_ROW = 16
N_COL = 8


def pick_slots(slot_key):
    return jax.random.permutation(slot_key, PRL)[:CRL]


def draw_child_update(key, part):
    order_len = CT * TILE
    sample = jnp.clip(jax.random.normal(key, (N_SUB, order_len, order_len), jnp.float32), -4.0, 4.0) * 0.7
    symmetric = (sample + jnp.swapaxes(sample, 1, 2)) * 0.5
    symmetric = symmetric.reshape(N_SUB, CRL, N_ROW, TILE, CCL, N_COL, TILE)
    symmetric = symmetric.transpose(0, 2, 1, 3, 5, 4, 6)
    return symmetric.reshape(N_SUB * order_len, order_len).astype(jnp.bfloat16)


def draw_parent_front(key, part):
    order_len = PT * TILE
    first_key, second_key = jax.random.split(key)
    sample = jnp.clip(jax.random.normal(first_key, (order_len, order_len), jnp.float32), -4.0, 4.0) * 0.7
    symmetric = (sample + sample.T) * 0.5
    diagonal = 64.0 * 4.0 ** jax.random.uniform(second_key, (order_len,), jnp.float32)
    diagonal_mask = jnp.arange(order_len)[:, None] == jnp.arange(order_len)[None, :]
    symmetric = jnp.where(diagonal_mask, diagonal[None, :], symmetric)
    symmetric = symmetric.reshape(PRL // PANEL, N_ROW, PANEL, TILE, order_len).transpose(1, 0, 2, 3, 4)
    return symmetric.reshape(order_len, order_len).astype(jnp.bfloat16)


def draw_tile_map(key, part):
    size_key, pick_key, full_key = jax.random.split(key, 3)
    least = max(1, CRL // 2)
    counts = jax.random.randint(size_key, (N_SUB,), least, CRL + 1)
    fullest = jax.random.randint(full_key, (), 0, N_SUB)
    counts = jnp.where(jnp.arange(N_SUB) == fullest, CRL, counts)
    slot_keys = jax.random.split(pick_key, N_SUB * N_ROW)
    slot_picks = jax.vmap(pick_slots)(slot_keys)
    slot_picks = slot_picks.reshape(N_SUB, N_ROW, CRL).transpose(0, 2, 1)
    residue = jnp.arange(N_ROW, dtype=jnp.int32)[None, None, :]
    targets = (slot_picks // PANEL * N_ROW + residue) * PANEL + slot_picks % PANEL
    live_mask = jnp.arange(CRL)[None, :, None] < counts[:, None, None]
    return jnp.where(live_mask, targets, -1).reshape(N_SUB, CT).astype(jnp.int32)


def setup_inputs(seed: int = 0) -> dict:
    key_list = jax.random.split(jax.random.key(seed), 4)
    return {
        "child_update": draw_child_update(jax.random.fold_in(key_list[3], 71), 0),
        "parent_front": draw_parent_front(jax.random.fold_in(key_list[3], 71), 0),
        "tile_map": draw_tile_map(jax.random.fold_in(key_list[3], 71), 0),
    }


def child_logical(stored_block):
    tile_grid = stored_block.reshape(N_ROW, CRL, TILE, N_COL, CCL, TILE)
    tile_grid = tile_grid.transpose(1, 0, 2, 4, 3, 5)
    return tile_grid.reshape(CT * TILE, CT * TILE)

def parent_logical(stored_front):
    order_len = PT * TILE
    grid = stored_front.reshape(N_ROW, PRL // PANEL, PANEL, TILE, order_len)
    return grid.transpose(1, 0, 2, 3, 4).reshape(order_len, order_len)

def parent_storage(logical_front):
    order_len = PT * TILE
    grid = logical_front.reshape(PRL // PANEL, N_ROW, PANEL, TILE, order_len)
    return grid.transpose(1, 0, 2, 3, 4).reshape(order_len, order_len)

def reference(child_update, parent_front, tile_map):
    order_len = PT * TILE
    panel_width = PANEL * TILE
    assembled = parent_logical(parent_front.astype(jnp.float32))
    inside = jnp.arange(TILE, dtype=jnp.int32)
    for child_index in range(N_SUB):
        stored_block = child_update[child_index * CT * TILE:(child_index + 1) * CT * TILE]
        update = child_logical(stored_block).astype(jnp.float32)
        targets = tile_map[child_index]
        element_rows = jnp.where(targets[:, None] >= 0, targets[:, None] * TILE + inside[None, :], order_len)
        element_rows = element_rows.reshape(-1).astype(jnp.int32)
        rows_placed = jnp.zeros((order_len, CT * TILE), jnp.float32).at[element_rows].add(update, mode='drop')
        assembled = assembled.at[:, element_rows].add(rows_placed, mode='drop')
    leading = assembled[:panel_width, :panel_width]
    lower_factor = jnp.tril(jnp.linalg.cholesky(leading))
    identity = jnp.eye(panel_width, dtype=jnp.float32)
    inverse = jax.scipy.linalg.solve_triangular(lower_factor, identity, lower=True)
    below_rows = jnp.dot(assembled[panel_width:, :panel_width].astype(jnp.float32), inverse.T.astype(jnp.float32), precision=lax.Precision.HIGHEST, preferred_element_type=jnp.float32)
    trailing = assembled[panel_width:, panel_width:] - jnp.dot(below_rows.astype(jnp.float32), below_rows.T.astype(jnp.float32), precision=lax.Precision.HIGHEST, preferred_element_type=jnp.float32)
    panel_col = jnp.concatenate([lower_factor, below_rows], axis=0)
    right_side = jnp.concatenate([assembled[:panel_width, panel_width:], trailing], axis=0)
    result = jnp.concatenate([panel_col, right_side], axis=1)
    return parent_storage(result)
```

```python
import functools

import jax
import jax.numpy as jnp
from jax import lax
from jax.experimental import pallas as pl
from jax.experimental.pallas import tpu as pltpu
from jax.sharding import PartitionSpec as P

TILE = 128
PANEL = 4
WIDTH = TILE * PANEL
MESH = pl.DeviceIdType.MESH
GROUP = 8
PIECE = WIDTH // GROUP


def remote(src, dst, send_sem, recv_sem, device):
    return pltpu.make_async_remote_copy(
        src_ref=src,
        dst_ref=dst,
        send_sem=send_sem,
        recv_sem=recv_sem,
        device_id=device,
        device_id_type=MESH,
    )


def each(count, skip, fn):
    def step(i, _):
        @pl.when(i != skip)
        def _():
            fn(i)

        return 0

    lax.fori_loop(0, count, step, 0)


def spread_kernel(
    n_sub,
    n_row,
    n_col,
    front,
    panel,
    top,
    lead,
    local_sem,
    top_send,
    top_cross,
    top_gather,
    top_recv,
    panel_send,
    panel_first,
    panel_recv,
    lead_sub,
    lead_col,
    lead_gather,
    lead_recv,
):
    s, r, c = lax.axis_index("sub"), lax.axis_index("row"), lax.axis_index("col")
    plane = n_sub * n_col
    p = s * n_col + c
    half, i = r // GROUP, r % GROUP
    depth = front.shape[0] // plane

    def at_plane(q):
        return (q // n_col, r, q % n_col)

    def at_group(j):
        return (s, half * GROUP + j, c)

    def top_piece(j):
        return top.at[pl.ds(pl.multiple_of(j * PIECE, PIECE), PIECE)]

    def lead_piece(j):
        return lead.at[pl.ds(pl.multiple_of(j * PIECE, PIECE), PIECE)]

    def panel_piece(q):
        return panel.at[pl.ds(pl.multiple_of(q * depth, depth), depth)]

    def front_piece(q):
        return front.at[pl.ds(pl.multiple_of(q * depth, depth), depth)]

    def front_top(j):
        return front.at[pl.ds(pl.multiple_of(j * PIECE, PIECE), PIECE)]

    barrier = pltpu.get_barrier_semaphore()
    across = (s, (1 - half) * GROUP + i, c)

    def greet(device):
        pl.semaphore_signal(barrier, inc=1, device_id=device, device_id_type=MESH)

    each(plane, p, lambda q: greet(at_plane(q)))
    each(GROUP, i, lambda j: greet(at_group(j)))
    greet(across)
    pl.semaphore_wait(barrier, plane - 1 + GROUP - 1 + 1)

    top_scatter = lambda j: remote(
        front_top(j), top_piece(j), top_send.at[j], top_recv.at[j], at_group(j)
    )
    panel_scatter = lambda q: remote(
        front_piece(q), panel_piece(q), panel_send.at[q], panel_recv.at[q], at_plane(q)
    )
    panel_zero = lambda q: remote(
        front_piece(0), panel_piece(0), panel_first.at[q], panel_recv.at[0], at_plane(q)
    )
    top_over = remote(top_piece(i), top_piece(i), top_cross, top_recv.at[i], across)
    top_share = lambda j: remote(
        top_piece(i), top_piece(i), top_gather.at[j], top_recv.at[i], at_group(j)
    )
    panel_share = lambda q: remote(
        panel_piece(p), panel_piece(p), panel_send.at[q], panel_recv.at[p], at_plane(q)
    )
    lead_down = lambda k: remote(
        top_piece(i), lead_piece(i), lead_sub.at[k], lead_recv.at[i], (k, r, 0)
    )
    lead_along = lambda k: remote(
        top_piece(i), lead_piece(i), lead_col.at[k], lead_recv.at[i], (s, r, k)
    )
    lead_forward = lambda k: remote(
        lead_piece(i), lead_piece(i), lead_col.at[k], lead_recv.at[i], (s, r, k)
    )
    lead_share = lambda j: remote(
        lead_piece(i), lead_piece(i), lead_gather.at[j], lead_recv.at[i], at_group(j)
    )
    own_top = pltpu.make_async_copy(front.at[pl.ds(0, WIDTH)], top, local_sem.at[0])
    own_panel = pltpu.make_async_copy(front, panel, local_sem.at[1])
    own_lead = pltpu.make_async_copy(top, lead, local_sem.at[2])

    def arrived(piece, sem):
        pltpu.make_async_copy(piece, piece, sem).wait()

    @pl.when(r == 0)
    def _():
        own_top.start()
        each(GROUP, 0, lambda j: top_scatter(j).start())

    @pl.when(p == 0)
    def _():
        own_panel.start()
        each(plane, 0, lambda q: panel_scatter(q).start())
        each(plane, 0, lambda q: panel_zero(q).start())

    @pl.when(r == 0)
    def _():
        own_top.wait()

    @pl.when(r != 0)
    def _():
        arrived(top_piece(i), top_recv.at[i])

    @pl.when(p == 0)
    def _():
        each(n_sub, 0, lambda k: lead_down(k).start())
        each(n_col, 0, lambda k: lead_along(k).start())

    @pl.when(half == 0)
    def _():
        top_over.start()
        each(GROUP, i, lambda j: pl.when(j != 0)(lambda: top_share(j).start()))

    @pl.when(half != 0)
    def _():
        each(GROUP, i, lambda j: top_share(j).start())

    @pl.when(p != 0)
    def _():
        arrived(panel_piece(p), panel_recv.at[p])
        each(plane, p, lambda q: pl.when(q != 0)(lambda: panel_share(q).start()))
        arrived(lead_piece(i), lead_recv.at[i])

        @pl.when(c == 0)
        def _():
            each(n_col, 0, lambda k: lead_forward(k).start())

        each(GROUP, i, lambda j: lead_share(j).start())

    @pl.when(r != 0)
    def _():
        each(GROUP, i, lambda j: arrived(top_piece(j), top_recv.at[j]))

    @pl.when(p == 0)
    def _():
        own_lead.start()

    @pl.when(p != 0)
    def _():
        each(GROUP, i, lambda j: arrived(lead_piece(j), lead_recv.at[j]))
        each(plane, p, lambda q: arrived(panel_piece(q), panel_recv.at[q]))

    @pl.when(r == 0)
    def _():
        each(GROUP, 0, lambda j: top_scatter(j).wait_send())

    @pl.when(half == 0)
    def _():
        top_over.wait_send()
        each(GROUP, i, lambda j: pl.when(j != 0)(lambda: top_share(j).wait_send()))

    @pl.when(half != 0)
    def _():
        each(GROUP, i, lambda j: top_share(j).wait_send())

    @pl.when(p == 0)
    def _():
        own_panel.wait()
        own_lead.wait()
        each(plane, 0, lambda q: panel_scatter(q).wait_send())
        each(plane, 0, lambda q: panel_zero(q).wait_send())
        each(n_sub, 0, lambda k: lead_down(k).wait_send())
        each(n_col, 0, lambda k: lead_along(k).wait_send())

    @pl.when(p != 0)
    def _():
        each(plane, p, lambda q: pl.when(q != 0)(lambda: panel_share(q).wait_send()))

        @pl.when(c == 0)
        def _():
            each(n_col, 0, lambda k: lead_forward(k).wait_send())

        each(GROUP, i, lambda j: lead_share(j).wait_send())


def spread_panels(front16, n_sub, n_row, n_col):
    rows, width = front16.shape
    vmem = pl.BlockSpec(memory_space=pltpu.VMEM)
    dma = pltpu.SemaphoreType.DMA
    plane = n_sub * n_col
    return pl.pallas_call(
        functools.partial(spread_kernel, n_sub, n_row, n_col),
        out_shape=(
            jax.ShapeDtypeStruct((rows, width), jnp.bfloat16),
            jax.ShapeDtypeStruct((WIDTH, width), jnp.bfloat16),
            jax.ShapeDtypeStruct((WIDTH, width), jnp.bfloat16),
        ),
        in_specs=[vmem],
        out_specs=(vmem, vmem, vmem),
        scratch_shapes=[
            dma((3,)),
            dma((GROUP,)),
            dma(()),
            dma((GROUP,)),
            dma((GROUP,)),
            dma((plane,)),
            dma((plane,)),
            dma((plane,)),
            dma((n_sub,)),
            dma((n_col,)),
            dma((GROUP,)),
            dma((GROUP,)),
        ],
        compiler_params=pltpu.CompilerParams(collective_id=0, has_side_effects=True),
        name="spread_panels",
    )(front16)


def invert_block(load_group, store_rows):
    sub = 8
    groups = TILE // sub
    lane = lax.broadcasted_iota(jnp.int32, (sub, TILE), 1)
    line = lax.broadcasted_iota(jnp.int32, (sub, TILE), 0)
    a = [load_group(g) for g in range(groups)]
    m = [jnp.where(lane == line + sub * g, 1.0, 0.0).astype(jnp.float32) for g in range(groups)]
    b = 4
    for j0 in range(0, TILE, b):
        g0, i0 = divmod(j0, sub)
        rows_a = [jnp.broadcast_to(a[g0][i0 + k : i0 + k + 1, :], (sub, TILE)) for k in range(b)]
        rows_m = [jnp.broadcast_to(m[g0][i0 + k : i0 + k + 1, :], (sub, TILE)) for k in range(b)]
        piv = [
            [
                jnp.broadcast_to(rows_a[l][:, j0 + k : j0 + k + 1], (sub, TILE))
                for k in range(l + 1)
            ]
            for l in range(b)
        ]
        low = [[None] * b for _ in range(b)]
        inv_diag = [None] * b
        for k in range(b):
            d = piv[k][k]
            for q in range(k):
                d = d - low[k][q] * low[k][q]
            inv_diag[k] = lax.rsqrt(d)
            for l in range(k + 1, b):
                v = piv[l][k]
                for q in range(k):
                    v = v - low[l][q] * low[k][q]
                low[l][k] = v * inv_diag[k]

        def solve(rows):
            out = []
            for l in range(b):
                v = rows[l]
                for q in range(l):
                    v = v - low[l][q] * out[q]
                out.append(v * inv_diag[l])
            return out

        def solve_back(rows):
            out = [None] * b
            for l in reversed(range(b)):
                v = rows[l]
                for q in range(l + 1, b):
                    v = v - low[q][l] * out[q]
                out[l] = v * inv_diag[l]
            return out

        x = solve(rows_m)
        store_rows(j0, x)
        if j0 + b == TILE:
            break
        va, vm = solve_back(solve(rows_a)), solve_back(x)
        first = (j0 + b) // sub
        for g in range(first, groups):
            for k in range(b):
                col = jnp.broadcast_to(a[g][:, j0 + k : j0 + k + 1], (sub, TILE))
                if g == g0:
                    col = jnp.where(line >= i0 + b, col, 0.0)
                if k == 0:
                    da, dm = col * va[0], col * vm[0]
                else:
                    da, dm = da + col * va[k], dm + col * vm[k]
            a[g], m[g] = a[g] - da, m[g] - dm


def split(x):
    high = x.astype(jnp.bfloat16)
    return high, (x - high.astype(jnp.float32)).astype(jnp.bfloat16)


def mul(x, y, transposed=False):
    dims = (((1,), (1 if transposed else 0,)), ((), ()))
    return lax.dot_general(x, y, dims, preferred_element_type=jnp.float32)


def mul3(x, y, transposed=False):
    xh, xl = split(x)
    yh, yl = split(y)
    return mul(xh, yh, transposed) + (mul(xh, yl, transposed) + mul(xl, yh, transposed))


def factor_kernel(lead, top, panel, front, out, work, inverse, lower, block_inv, right):
    row_id = lax.axis_index("row")
    block_id = lax.axis_index("sub") * lax.axis_size("col") + lax.axis_index("col")
    width = WIDTH
    work[...] = lead[...].astype(jnp.float32)
    row_of = lax.broadcasted_iota(jnp.int32, (width, width), 0)
    col_of = lax.broadcasted_iota(jnp.int32, (width, width), 1)
    inverse[...] = jnp.where(row_of == col_of, 1.0, 0.0).astype(jnp.float32)
    lower[...] = jnp.zeros_like(lower)

    for kb in range(PANEL):
        o = kb * TILE

        def load_group(g):
            return work[o + 8 * g : o + 8 * g + 8, o : o + TILE]

        def store_rows(j0, x):
            for k in range(len(x)):
                block_inv[j0 + k : j0 + k + 1, :] = x[k][0:1, :]

        invert_block(load_group, store_rows)
        d_inv = block_inv[...]
        rest = width - o - TILE
        diag = mul3(work[o : o + TILE, o : o + TILE], d_inv, True)
        tri = lax.broadcasted_iota(jnp.int32, (TILE, TILE), 0) >= lax.broadcasted_iota(
            jnp.int32, (TILE, TILE), 1
        )
        lower[o : o + TILE, o : o + TILE] = jnp.where(tri, diag, 0.0)
        x_rows = mul3(d_inv, inverse[o : o + TILE, 0 : o + TILE])
        inverse[o : o + TILE, 0 : o + TILE] = x_rows
        if rest:
            below = mul3(work[o + TILE :, o : o + TILE], d_inv, True)
            lower[o + TILE :, o : o + TILE] = below
            work[o + TILE :, o + TILE :] = work[o + TILE :, o + TILE :] - mul3(below, below, True)
            inverse[o + TILE :, 0 : o + TILE] = inverse[o + TILE :, 0 : o + TILE] - mul3(
                below, x_rows
            )

    inv_high, inv_low = split(inverse[...])
    tops = top[...]
    right[...] = mul(inv_high, tops) + mul(inv_low, tops)
    chunk = 128

    @pl.loop(0, panel.shape[0] // chunk)
    def _(t):
        rows = pl.ds(pl.multiple_of(t * chunk, chunk), chunk)
        a_rows = panel[rows, :]
        xh, xl = split(inverse[...])
        f_rows = mul(a_rows, xh, True) + mul(a_rows, xl, True)
        head = (row_id == 0) & (t < width // chunk)

        @pl.when(block_id == 0)
        def _():
            out[rows, :] = f_rows

            @pl.when(head)
            def _():
                out[rows, :] = lower[rows, :]

        @pl.when(block_id != 0)
        def _():
            @pl.when(head)
            def _():
                out[rows, :] = front[rows, :]

            @pl.when(jnp.logical_not(head))
            def _():
                out[rows, :] = front[rows, :] - mul3(f_rows, right[...])


def factor_and_update(lead, top, panel, front):
    vmem = pl.BlockSpec(memory_space=pltpu.VMEM)
    return pl.pallas_call(
        factor_kernel,
        out_shape=jax.ShapeDtypeStruct(front.shape, jnp.float32),
        in_specs=[vmem] * 4,
        out_specs=vmem,
        scratch_shapes=[
            pltpu.VMEM((WIDTH, WIDTH), jnp.float32),
            pltpu.VMEM((WIDTH, WIDTH), jnp.float32),
            pltpu.VMEM((WIDTH, WIDTH), jnp.float32),
            pltpu.VMEM((TILE, TILE), jnp.float32),
            pltpu.VMEM((WIDTH, WIDTH), jnp.float32),
        ],
        name="factor_and_update",
    )(lead, top, panel, front)


def body(child_update, parent_front, tile_map):
    tile_len = TILE
    panel_tiles = PANEL
    sub_count = lax.axis_size("sub")
    row_count = lax.axis_size("row")
    col_count = lax.axis_size("col")
    sub_id = lax.axis_index("sub")
    row_id = lax.axis_index("row")
    col_id = lax.axis_index("col")
    child_rows = child_update.shape[0] // tile_len
    child_cols = child_update.shape[1] // tile_len
    front_rows = parent_front.shape[0] // tile_len
    own_map = lax.dynamic_index_in_dim(tile_map, sub_id, 0, keepdims=False)
    own_cols = lax.dynamic_index_in_dim(
        own_map.reshape(child_cols, col_count), col_id, 1, keepdims=False
    )
    live_cols = own_cols >= 0
    destination = jnp.floor_divide(jnp.floor_divide(own_cols, panel_tiles), col_count)
    slot_index = jnp.remainder(own_cols, panel_tiles)
    dest_hit = destination[None, :] == jnp.arange(sub_count, dtype=jnp.int32)[:, None]
    slot_hit = slot_index[None, :] == jnp.arange(panel_tiles, dtype=jnp.int32)[:, None]
    select = (live_cols[None, None, :] & dest_hit[:, None, :] & slot_hit[None, :, :]).astype(
        jnp.bfloat16
    )
    column_slabs = child_update.reshape(child_rows * tile_len, child_cols, tile_len)
    payload = jnp.einsum(
        "dqk,rky->dqry", select, column_slabs, preferred_element_type=jnp.float32
    ).astype(jnp.bfloat16)
    maps_rows = lax.dynamic_index_in_dim(
        tile_map.reshape(sub_count, child_rows, row_count), row_id, 2, keepdims=False
    )
    local_row = jnp.floor_divide(
        jnp.floor_divide(maps_rows, panel_tiles), row_count
    ) * panel_tiles + jnp.remainder(maps_rows, panel_tiles)
    row_hit = (maps_rows[:, :, None] >= 0) & (
        local_row[:, :, None] == jnp.arange(front_rows, dtype=jnp.int32)[None, None, :]
    )
    place_row = row_hit.astype(jnp.bfloat16)
    arrived = lax.all_to_all(payload, "sub", split_axis=0, concat_axis=0, tiled=True)
    slot_count = arrived.shape[1]
    grid = arrived.reshape(sub_count, slot_count, child_rows, tile_len, tile_len)
    spread = jnp.einsum("ska,sqkyx->ayqx", place_row, grid, preferred_element_type=jnp.float32)
    placed = spread.reshape(front_rows * tile_len, slot_count * tile_len)
    front_local = parent_front.astype(jnp.float32) + placed
    panel, top, lead = spread_panels(
        front_local.astype(jnp.bfloat16), sub_count, row_count, col_count
    )
    return factor_and_update(lead, top, panel, front_local)


def solution(mesh):
    in_specs = (P(("sub", "row"), "col"), P("row", ("sub", "col")), P())
    out_specs = P("row", ("sub", "col"))
    return jax.shard_map(body, mesh=mesh, in_specs=in_specs, out_specs=out_specs, check_vma=False)
```

```python
import functools

import jax
import jax.numpy as jnp
from jax import lax
from jax.experimental import pallas as pl
from jax.experimental.pallas import tpu as pltpu
from jax.sharding import PartitionSpec as P

TILE = 128
PANEL = 4
WIDTH = TILE * PANEL
MESH = pl.DeviceIdType.MESH
GROUP = 8
PIECE = WIDTH // GROUP


def remote(src, dst, send_sem, recv_sem, device):
    return pltpu.make_async_remote_copy(
        src_ref=src,
        dst_ref=dst,
        send_sem=send_sem,
        recv_sem=recv_sem,
        device_id=device,
        device_id_type=MESH,
    )


def each(count, skip, fn):
    def step(i, _):
        @pl.when(i != skip)
        def _():
            fn(i)

        return 0

    lax.fori_loop(0, count, step, 0)


def spread_kernel(
    n_sub,
    n_row,
    n_col,
    front,
    panel,
    top,
    inv_high,
    inv_low,
    lower,
    lead,
    work,
    inverse,
    block_inv,
    local_sem,
    top_send,
    top_cross,
    top_gather,
    top_recv,
    panel_send,
    panel_first,
    panel_recv,
    lead_sub,
    lead_col,
    lead_gather,
    lead_recv,
):
    s, r, c = lax.axis_index("sub"), lax.axis_index("row"), lax.axis_index("col")
    plane = n_sub * n_col
    p = s * n_col + c
    half, i = r // GROUP, r % GROUP
    depth = front.shape[0] // plane

    def at_plane(q):
        return (q // n_col, r, q % n_col)

    def at_group(j):
        return (s, half * GROUP + j, c)

    def top_piece(j):
        return top.at[pl.ds(pl.multiple_of(j * PIECE, PIECE), PIECE)]

    def lead_piece(j):
        return lead.at[pl.ds(pl.multiple_of(j * PIECE, PIECE), PIECE)]

    def panel_piece(q):
        return panel.at[pl.ds(pl.multiple_of(q * depth, depth), depth)]

    def front_piece(q):
        return front.at[pl.ds(pl.multiple_of(q * depth, depth), depth)]

    def front_top(j):
        return front.at[pl.ds(pl.multiple_of(j * PIECE, PIECE), PIECE)]

    barrier = pltpu.get_barrier_semaphore()
    across = (s, (1 - half) * GROUP + i, c)

    def greet(device):
        pl.semaphore_signal(barrier, inc=1, device_id=device, device_id_type=MESH)

    each(plane, p, lambda q: greet(at_plane(q)))
    each(GROUP, i, lambda j: greet(at_group(j)))
    greet(across)
    pl.semaphore_wait(barrier, plane - 1 + GROUP - 1 + 1)

    top_scatter = lambda j: remote(
        front_top(j), top_piece(j), top_send.at[j], top_recv.at[j], at_group(j)
    )
    panel_scatter = lambda q: remote(
        front_piece(q), panel_piece(q), panel_send.at[q], panel_recv.at[q], at_plane(q)
    )
    panel_zero = lambda q: remote(
        front_piece(0), panel_piece(0), panel_first.at[q], panel_recv.at[0], at_plane(q)
    )
    top_over = remote(top_piece(i), top_piece(i), top_cross, top_recv.at[i], across)
    top_share = lambda j: remote(
        top_piece(i), top_piece(i), top_gather.at[j], top_recv.at[i], at_group(j)
    )
    panel_share = lambda q: remote(
        panel_piece(p), panel_piece(p), panel_send.at[q], panel_recv.at[p], at_plane(q)
    )
    lead_down = lambda k: remote(
        top_piece(i), lead_piece(i), lead_sub.at[k], lead_recv.at[i], (k, r, 0)
    )
    lead_along = lambda k: remote(
        top_piece(i), lead_piece(i), lead_col.at[k], lead_recv.at[i], (s, r, k)
    )
    lead_forward = lambda k: remote(
        lead_piece(i), lead_piece(i), lead_col.at[k], lead_recv.at[i], (s, r, k)
    )
    lead_share = lambda j: remote(
        lead_piece(i), lead_piece(i), lead_gather.at[j], lead_recv.at[i], at_group(j)
    )
    own_top = pltpu.make_async_copy(front.at[pl.ds(0, WIDTH)], top, local_sem.at[0])
    own_panel = pltpu.make_async_copy(front, panel, local_sem.at[1])
    own_lead = pltpu.make_async_copy(top, lead, local_sem.at[2])

    def arrived(piece, sem):
        pltpu.make_async_copy(piece, piece, sem).wait()

    @pl.when(r == 0)
    def _():
        own_top.start()
        each(GROUP, 0, lambda j: top_scatter(j).start())

    @pl.when(r == 0)
    def _():
        own_top.wait()

    @pl.when(r != 0)
    def _():
        arrived(top_piece(i), top_recv.at[i])

    @pl.when(p == 0)
    def _():
        each(n_sub, 0, lambda k: lead_down(k).start())
        each(n_col, 0, lambda k: lead_along(k).start())
        own_panel.start()
        each(plane, 0, lambda q: panel_scatter(q).start())
        each(plane, 0, lambda q: panel_zero(q).start())

    @pl.when(half == 0)
    def _():
        top_over.start()
        each(GROUP, i, lambda j: pl.when(j != 0)(lambda: top_share(j).start()))

    @pl.when(half != 0)
    def _():
        each(GROUP, i, lambda j: top_share(j).start())

    @pl.when(p != 0)
    def _():
        arrived(panel_piece(p), panel_recv.at[p])
        each(plane, p, lambda q: pl.when(q != 0)(lambda: panel_share(q).start()))
        arrived(lead_piece(i), lead_recv.at[i])

        @pl.when(c == 0)
        def _():
            each(n_col, 0, lambda k: lead_forward(k).start())

        each(GROUP, i, lambda j: lead_share(j).start())

    @pl.when(r != 0)
    def _():
        each(GROUP, i, lambda j: arrived(top_piece(j), top_recv.at[j]))

    @pl.when(p == 0)
    def _():
        own_lead.start()
        own_lead.wait()

    @pl.when(p != 0)
    def _():
        each(GROUP, i, lambda j: arrived(lead_piece(j), lead_recv.at[j]))

    factor_leading(lead, work, inverse, lower, block_inv, inv_high, inv_low)

    @pl.when(p != 0)
    def _():
        each(plane, p, lambda q: arrived(panel_piece(q), panel_recv.at[q]))

    @pl.when(r == 0)
    def _():
        each(GROUP, 0, lambda j: top_scatter(j).wait_send())

    @pl.when(half == 0)
    def _():
        top_over.wait_send()
        each(GROUP, i, lambda j: pl.when(j != 0)(lambda: top_share(j).wait_send()))

    @pl.when(half != 0)
    def _():
        each(GROUP, i, lambda j: top_share(j).wait_send())

    @pl.when(p == 0)
    def _():
        own_panel.wait()
        each(plane, 0, lambda q: panel_scatter(q).wait_send())
        each(plane, 0, lambda q: panel_zero(q).wait_send())
        each(n_sub, 0, lambda k: lead_down(k).wait_send())
        each(n_col, 0, lambda k: lead_along(k).wait_send())

    @pl.when(p != 0)
    def _():
        each(plane, p, lambda q: pl.when(q != 0)(lambda: panel_share(q).wait_send()))

        @pl.when(c == 0)
        def _():
            each(n_col, 0, lambda k: lead_forward(k).wait_send())

        each(GROUP, i, lambda j: lead_share(j).wait_send())


def spread_panels(front16, n_sub, n_row, n_col):
    rows, width = front16.shape
    vmem = pl.BlockSpec(memory_space=pltpu.VMEM)
    dma = pltpu.SemaphoreType.DMA
    plane = n_sub * n_col
    return pl.pallas_call(
        functools.partial(spread_kernel, n_sub, n_row, n_col),
        out_shape=(
            jax.ShapeDtypeStruct((rows, width), jnp.bfloat16),
            jax.ShapeDtypeStruct((WIDTH, width), jnp.bfloat16),
            jax.ShapeDtypeStruct((WIDTH, WIDTH), jnp.bfloat16),
            jax.ShapeDtypeStruct((WIDTH, WIDTH), jnp.bfloat16),
            jax.ShapeDtypeStruct((WIDTH, WIDTH), jnp.float32),
        ),
        in_specs=[vmem],
        out_specs=(vmem,) * 5,
        scratch_shapes=[
            pltpu.VMEM((WIDTH, WIDTH), jnp.bfloat16),
            pltpu.VMEM((WIDTH, WIDTH), jnp.float32),
            pltpu.VMEM((WIDTH, WIDTH), jnp.float32),
            pltpu.VMEM((TILE, TILE), jnp.float32),
            dma((3,)),
            dma((GROUP,)),
            dma(()),
            dma((GROUP,)),
            dma((GROUP,)),
            dma((plane,)),
            dma((plane,)),
            dma((plane,)),
            dma((n_sub,)),
            dma((n_col,)),
            dma((GROUP,)),
            dma((GROUP,)),
        ],
        compiler_params=pltpu.CompilerParams(collective_id=0, has_side_effects=True),
        name="spread_panels",
    )(front16)


def invert_block(block, store_rows):
    sub = 8
    b = 4
    line = lax.broadcasted_iota(jnp.int32, (TILE, TILE), 0)
    lane = lax.broadcasted_iota(jnp.int32, (TILE, TILE), 1)
    a = block
    m = jnp.where(lane == line, 1.0, 0.0).astype(jnp.float32)
    done = 0
    for j0 in range(0, TILE, b):
        i0 = j0 - done
        rows_a = [jnp.broadcast_to(a[i0 + k : i0 + k + 1, :], (sub, TILE)) for k in range(b)]
        rows_m = [jnp.broadcast_to(m[i0 + k : i0 + k + 1, :], (sub, TILE)) for k in range(b)]
        piv = [
            [
                jnp.broadcast_to(rows_a[l][:, j0 + k : j0 + k + 1], (sub, TILE))
                for k in range(l + 1)
            ]
            for l in range(b)
        ]
        low = [[None] * b for _ in range(b)]
        inv_diag = [None] * b
        for k in range(b):
            d = piv[k][k]
            for q in range(k):
                d = d - low[k][q] * low[k][q]
            inv_diag[k] = lax.rsqrt(d)
            for l in range(k + 1, b):
                v = piv[l][k]
                for q in range(k):
                    v = v - low[l][q] * low[k][q]
                low[l][k] = v * inv_diag[k]

        def solve(rows):
            out = []
            for l in range(b):
                v = rows[l]
                for q in range(l):
                    v = v - low[l][q] * out[q]
                out.append(v * inv_diag[l])
            return out

        def solve_back(rows):
            out = [None] * b
            for l in reversed(range(b)):
                v = rows[l]
                for q in range(l + 1, b):
                    v = v - low[q][l] * out[q]
                out[l] = v * inv_diag[l]
            return out

        x = solve(rows_m)
        store_rows(j0, x)
        if j0 + b == TILE:
            break
        va, vm = solve_back(solve(rows_a)), solve_back(x)
        drop = (j0 + b) // sub * sub - done
        if drop:
            a, m, done = a[drop:], m[drop:], done + drop
        height = TILE - done
        da = dm = None
        for k in range(b):
            col = jnp.broadcast_to(a[:, j0 + k : j0 + k + 1], (height, TILE))
            if done < j0 + b:
                col = jnp.where(line[:height] >= j0 + b - done, col, 0.0)
            ta = col * jnp.broadcast_to(va[k][0:1], (height, TILE))
            tm = col * jnp.broadcast_to(vm[k][0:1], (height, TILE))
            da, dm = (ta, tm) if k == 0 else (da + ta, dm + tm)
        a, m = a - da, m - dm


def split(x):
    high = x.astype(jnp.bfloat16)
    return high, (x - high.astype(jnp.float32)).astype(jnp.bfloat16)


def mul(x, y, transposed=False):
    dims = (((1,), (1 if transposed else 0,)), ((), ()))
    return lax.dot_general(x, y, dims, preferred_element_type=jnp.float32)


def mul3(x, y, transposed=False):
    xh, xl = split(x)
    yh, yl = split(y)
    return mul(xh, yh, transposed) + (mul(xh, yl, transposed) + mul(xl, yh, transposed))


def factor_leading(lead, work, inverse, lower, block_inv, inv_high, inv_low):
    width = WIDTH
    work[...] = lead[...].astype(jnp.float32)
    row_of = lax.broadcasted_iota(jnp.int32, (width, width), 0)
    col_of = lax.broadcasted_iota(jnp.int32, (width, width), 1)
    inverse[...] = jnp.where(row_of == col_of, 1.0, 0.0).astype(jnp.float32)

    def store_rows(j0, x):
        for k in range(len(x)):
            block_inv[j0 + k : j0 + k + 1, :] = x[k][0:1, :]

    def step(kb, _):
        o = pl.multiple_of(kb * TILE, TILE)
        here = pl.ds(o, TILE)
        invert_block(work[here, here], store_rows)
        d_inv = block_inv[...]
        below = mul3(work[:, here], d_inv, True)
        line = lax.broadcasted_iota(jnp.int32, (width, TILE), 0)
        lane = lax.broadcasted_iota(jnp.int32, (width, TILE), 1)
        lower[:, here] = jnp.where(line >= lane + o, below, 0.0)
        below = jnp.where(line >= o + TILE, below, 0.0)
        x_rows = mul3(d_inv, inverse[here, :])
        inverse[here, :] = x_rows
        work[...] = work[...] - mul3(below, below, True)
        inverse[...] = inverse[...] - mul3(below, x_rows)
        return 0

    lax.fori_loop(0, PANEL, step, 0)
    high, low = split(inverse[...])
    inv_high[...] = high
    inv_low[...] = low


def update_kernel(inv_high, inv_low, lower, top, panel, front, out, right):
    row_id = lax.axis_index("row")
    block_id = lax.axis_index("sub") * lax.axis_size("col") + lax.axis_index("col")
    tops = top[...]
    right[...] = mul(inv_high[...], tops) + mul(inv_low[...], tops)
    chunk = 128

    @pl.loop(0, panel.shape[0] // chunk)
    def _(t):
        rows = pl.ds(pl.multiple_of(t * chunk, chunk), chunk)
        a_rows = panel[rows, :]
        f_rows = mul(a_rows, inv_high[...], True) + mul(a_rows, inv_low[...], True)
        head = (row_id == 0) & (t < WIDTH // chunk)

        @pl.when(block_id == 0)
        def _():
            out[rows, :] = f_rows

            @pl.when(head)
            def _():
                out[rows, :] = lower[rows, :]

        @pl.when(block_id != 0)
        def _():
            @pl.when(head)
            def _():
                out[rows, :] = front[rows, :]

            @pl.when(jnp.logical_not(head))
            def _():
                out[rows, :] = front[rows, :] - mul3(f_rows, right[...])


def apply_update(inv_high, inv_low, lower, top, panel, front):
    vmem = pl.BlockSpec(memory_space=pltpu.VMEM)
    return pl.pallas_call(
        update_kernel,
        out_shape=jax.ShapeDtypeStruct(front.shape, jnp.float32),
        in_specs=[vmem] * 6,
        out_specs=vmem,
        scratch_shapes=[pltpu.VMEM((WIDTH, WIDTH), jnp.float32)],
        name="apply_update",
    )(inv_high, inv_low, lower, top, panel, front)


def body(child_update, parent_front, tile_map):
    tile_len = TILE
    panel_tiles = PANEL
    sub_count = lax.axis_size("sub")
    row_count = lax.axis_size("row")
    col_count = lax.axis_size("col")
    sub_id = lax.axis_index("sub")
    row_id = lax.axis_index("row")
    col_id = lax.axis_index("col")
    child_rows = child_update.shape[0] // tile_len
    child_cols = child_update.shape[1] // tile_len
    front_rows = parent_front.shape[0] // tile_len
    own_map = lax.dynamic_index_in_dim(tile_map, sub_id, 0, keepdims=False)
    own_cols = lax.dynamic_index_in_dim(
        own_map.reshape(child_cols, col_count), col_id, 1, keepdims=False
    )
    live_cols = own_cols >= 0
    destination = jnp.floor_divide(jnp.floor_divide(own_cols, panel_tiles), col_count)
    slot_index = jnp.remainder(own_cols, panel_tiles)
    dest_hit = destination[None, :] == jnp.arange(sub_count, dtype=jnp.int32)[:, None]
    slot_hit = slot_index[None, :] == jnp.arange(panel_tiles, dtype=jnp.int32)[:, None]
    select = (live_cols[None, None, :] & dest_hit[:, None, :] & slot_hit[None, :, :]).astype(
        jnp.bfloat16
    )
    column_slabs = child_update.reshape(child_rows * tile_len, child_cols, tile_len)
    payload = jnp.einsum(
        "dqk,rky->dqry", select, column_slabs, preferred_element_type=jnp.float32
    ).astype(jnp.bfloat16)
    maps_rows = lax.dynamic_index_in_dim(
        tile_map.reshape(sub_count, child_rows, row_count), row_id, 2, keepdims=False
    )
    local_row = jnp.floor_divide(
        jnp.floor_divide(maps_rows, panel_tiles), row_count
    ) * panel_tiles + jnp.remainder(maps_rows, panel_tiles)
    row_hit = (maps_rows[:, :, None] >= 0) & (
        local_row[:, :, None] == jnp.arange(front_rows, dtype=jnp.int32)[None, None, :]
    )
    place_row = row_hit.astype(jnp.bfloat16)
    arrived = lax.all_to_all(payload, "sub", split_axis=0, concat_axis=0, tiled=True)
    slot_count = arrived.shape[1]
    grid = arrived.reshape(sub_count, slot_count, child_rows, tile_len, tile_len)
    spread = jnp.einsum("ska,sqkyx->ayqx", place_row, grid, preferred_element_type=jnp.float32)
    placed = spread.reshape(front_rows * tile_len, slot_count * tile_len)
    front_local = parent_front.astype(jnp.float32) + placed
    panel, top, inv_high, inv_low, lower = spread_panels(
        front_local.astype(jnp.bfloat16), sub_count, row_count, col_count
    )
    return apply_update(inv_high, inv_low, lower, top, panel, front_local)


def solution(mesh):
    in_specs = (P(("sub", "row"), "col"), P("row", ("sub", "col")), P())
    out_specs = P("row", ("sub", "col"))
    return jax.shard_map(body, mesh=mesh, in_specs=in_specs, out_specs=out_specs, check_vma=False)
```

```python
import functools

import jax
import jax.numpy as jnp
from jax import lax
from jax.experimental import pallas as pl
from jax.experimental.pallas import tpu as pltpu
from jax.sharding import PartitionSpec as P

TILE = 128
PANEL = 4
WIDTH = TILE * PANEL
MESH = pl.DeviceIdType.MESH
GROUP = 8
PIECE = WIDTH // GROUP


def remote(src, dst, send_sem, recv_sem, device):
    return pltpu.make_async_remote_copy(
        src_ref=src,
        dst_ref=dst,
        send_sem=send_sem,
        recv_sem=recv_sem,
        device_id=device,
        device_id_type=MESH,
    )


def each(count, skip, fn):
    def step(i, _):
        @pl.when(i != skip)
        def _():
            fn(i)

        return 0

    lax.fori_loop(0, count, step, 0)


def spread_kernel(
    n_sub,
    n_row,
    n_col,
    front,
    panel,
    top,
    inv_high,
    inv_low,
    lower,
    lead,
    work,
    inverse,
    block_inv,
    local_sem,
    top_send,
    top_cross,
    top_gather,
    top_recv,
    panel_send,
    panel_first,
    panel_recv,
    lead_sub,
    lead_col,
    lead_gather,
    lead_recv,
):
    s, r, c = lax.axis_index("sub"), lax.axis_index("row"), lax.axis_index("col")
    plane = n_sub * n_col
    p = s * n_col + c
    half, i = r // GROUP, r % GROUP
    depth = front.shape[0] // plane

    def at_plane(q):
        return (q // n_col, r, q % n_col)

    def at_group(j):
        return (s, half * GROUP + j, c)

    def top_piece(j):
        return top.at[pl.ds(pl.multiple_of(j * PIECE, PIECE), PIECE)]

    def lead_piece(j):
        return lead.at[pl.ds(pl.multiple_of(j * PIECE, PIECE), PIECE)]

    def panel_piece(q):
        return panel.at[pl.ds(pl.multiple_of(q * depth, depth), depth)]

    def front_piece(q):
        return front.at[pl.ds(pl.multiple_of(q * depth, depth), depth)]

    def front_top(j):
        return front.at[pl.ds(pl.multiple_of(j * PIECE, PIECE), PIECE)]

    barrier = pltpu.get_barrier_semaphore()
    across = (s, (1 - half) * GROUP + i, c)

    def greet(device):
        pl.semaphore_signal(barrier, inc=1, device_id=device, device_id_type=MESH)

    each(plane, p, lambda q: greet(at_plane(q)))
    each(GROUP, i, lambda j: greet(at_group(j)))
    greet(across)
    pl.semaphore_wait(barrier, plane - 1 + GROUP - 1 + 1)

    top_scatter = lambda j: remote(
        front_top(j), top_piece(j), top_send.at[j], top_recv.at[j], at_group(j)
    )
    panel_scatter = lambda q: remote(
        front_piece(q), panel_piece(q), panel_send.at[q], panel_recv.at[q], at_plane(q)
    )
    panel_zero = lambda q: remote(
        front_piece(0), panel_piece(0), panel_first.at[q], panel_recv.at[0], at_plane(q)
    )
    top_over = remote(top_piece(i), top_piece(i), top_cross, top_recv.at[i], across)
    top_share = lambda j: remote(
        top_piece(i), top_piece(i), top_gather.at[j], top_recv.at[i], at_group(j)
    )
    panel_share = lambda q: remote(
        panel_piece(p), panel_piece(p), panel_send.at[q], panel_recv.at[p], at_plane(q)
    )
    lead_down = lambda k: remote(
        top_piece(i), lead_piece(i), lead_sub.at[k], lead_recv.at[i], (k, r, 0)
    )
    lead_along = lambda k: remote(
        top_piece(i), lead_piece(i), lead_col.at[k], lead_recv.at[i], (s, r, k)
    )
    lead_forward = lambda k: remote(
        lead_piece(i), lead_piece(i), lead_col.at[k], lead_recv.at[i], (s, r, k)
    )
    lead_share = lambda j: remote(
        lead_piece(i), lead_piece(i), lead_gather.at[j], lead_recv.at[i], at_group(j)
    )
    own_top = pltpu.make_async_copy(front.at[pl.ds(0, WIDTH)], top, local_sem.at[0])
    own_panel = pltpu.make_async_copy(front, panel, local_sem.at[1])
    own_lead = pltpu.make_async_copy(top, lead, local_sem.at[2])

    def arrived(piece, sem):
        pltpu.make_async_copy(piece, piece, sem).wait()

    def share_top():
        each(GROUP, i, lambda j: pl.when((j != 0) | (half != 0))(lambda: top_share(j).start()))

    @pl.when(r == 0)
    def _():
        own_top.start()
        each(GROUP, 0, lambda j: top_scatter(j).start())
        own_top.wait()

    @pl.when((r != 0) & (half == 0))
    def _():
        arrived(top_piece(i), top_recv.at[i])

    @pl.when(half == 0)
    def _():
        top_over.start()

    @pl.when(p == 0)
    def _():
        @pl.when(half != 0)
        def _():
            arrived(top_piece(i), top_recv.at[i])

        each(n_sub, 0, lambda k: lead_down(k).start())
        each(n_col, 0, lambda k: lead_along(k).start())
        own_panel.start()
        each(plane, 0, lambda q: panel_scatter(q).start())
        share_top()
        each(plane, 0, lambda q: panel_zero(q).start())

    @pl.when(p != 0)
    def _():
        arrived(lead_piece(i), lead_recv.at[i])

        @pl.when(c == 0)
        def _():
            each(n_col, 0, lambda k: lead_forward(k).start())

        each(GROUP, i, lambda j: lead_share(j).start())

        @pl.when(half != 0)
        def _():
            arrived(top_piece(i), top_recv.at[i])

        share_top()
        arrived(panel_piece(p), panel_recv.at[p])
        each(plane, p, lambda q: pl.when(q != 0)(lambda: panel_share(q).start()))

    @pl.when(r != 0)
    def _():
        each(GROUP, i, lambda j: arrived(top_piece(j), top_recv.at[j]))

    @pl.when(p == 0)
    def _():
        own_lead.start()
        own_lead.wait()

    @pl.when(p != 0)
    def _():
        each(GROUP, i, lambda j: arrived(lead_piece(j), lead_recv.at[j]))

    factor_leading(lead, work, inverse, lower, block_inv, inv_high, inv_low)

    @pl.when(p != 0)
    def _():
        each(plane, p, lambda q: arrived(panel_piece(q), panel_recv.at[q]))

    @pl.when(r == 0)
    def _():
        each(GROUP, 0, lambda j: top_scatter(j).wait_send())

    @pl.when(half == 0)
    def _():
        top_over.wait_send()
        each(GROUP, i, lambda j: pl.when(j != 0)(lambda: top_share(j).wait_send()))

    @pl.when(half != 0)
    def _():
        each(GROUP, i, lambda j: top_share(j).wait_send())

    @pl.when(p == 0)
    def _():
        own_panel.wait()
        each(plane, 0, lambda q: panel_scatter(q).wait_send())
        each(plane, 0, lambda q: panel_zero(q).wait_send())
        each(n_sub, 0, lambda k: lead_down(k).wait_send())
        each(n_col, 0, lambda k: lead_along(k).wait_send())

    @pl.when(p != 0)
    def _():
        each(plane, p, lambda q: pl.when(q != 0)(lambda: panel_share(q).wait_send()))

        @pl.when(c == 0)
        def _():
            each(n_col, 0, lambda k: lead_forward(k).wait_send())

        each(GROUP, i, lambda j: lead_share(j).wait_send())


def spread_panels(front16, n_sub, n_row, n_col):
    rows, width = front16.shape
    vmem = pl.BlockSpec(memory_space=pltpu.VMEM)
    dma = pltpu.SemaphoreType.DMA
    plane = n_sub * n_col
    return pl.pallas_call(
        functools.partial(spread_kernel, n_sub, n_row, n_col),
        out_shape=(
            jax.ShapeDtypeStruct((rows, width), jnp.bfloat16),
            jax.ShapeDtypeStruct((WIDTH, width), jnp.bfloat16),
            jax.ShapeDtypeStruct((WIDTH, WIDTH), jnp.bfloat16),
            jax.ShapeDtypeStruct((WIDTH, WIDTH), jnp.bfloat16),
            jax.ShapeDtypeStruct((WIDTH, WIDTH), jnp.float32),
        ),
        in_specs=[vmem],
        out_specs=(vmem,) * 5,
        scratch_shapes=[
            pltpu.VMEM((WIDTH, WIDTH), jnp.bfloat16),
            pltpu.VMEM((WIDTH, WIDTH), jnp.float32),
            pltpu.VMEM((WIDTH, WIDTH), jnp.float32),
            pltpu.VMEM((TILE, TILE), jnp.float32),
            dma((3,)),
            dma((GROUP,)),
            dma(()),
            dma((GROUP,)),
            dma((GROUP,)),
            dma((plane,)),
            dma((plane,)),
            dma((plane,)),
            dma((n_sub,)),
            dma((n_col,)),
            dma((GROUP,)),
            dma((GROUP,)),
        ],
        compiler_params=pltpu.CompilerParams(collective_id=0, has_side_effects=True),
        name="spread_panels",
    )(front16)


def invert_block(block, store_rows):
    sub = 8
    b = 4
    line = lax.broadcasted_iota(jnp.int32, (TILE, TILE), 0)
    lane = lax.broadcasted_iota(jnp.int32, (TILE, TILE), 1)
    a = block
    m = jnp.where(lane == line, 1.0, 0.0).astype(jnp.float32)
    done = 0
    for j0 in range(0, TILE, b):
        i0 = j0 - done
        rows_a = [jnp.broadcast_to(a[i0 + k : i0 + k + 1, :], (sub, TILE)) for k in range(b)]
        rows_m = [jnp.broadcast_to(m[i0 + k : i0 + k + 1, :], (sub, TILE)) for k in range(b)]
        piv = [
            [
                jnp.broadcast_to(rows_a[l][:, j0 + k : j0 + k + 1], (sub, TILE))
                for k in range(l + 1)
            ]
            for l in range(b)
        ]
        low = [[None] * b for _ in range(b)]
        inv_diag = [None] * b
        for k in range(b):
            d = piv[k][k]
            for q in range(k):
                d = d - low[k][q] * low[k][q]
            inv_diag[k] = lax.rsqrt(d)
            for l in range(k + 1, b):
                v = piv[l][k]
                for q in range(k):
                    v = v - low[l][q] * low[k][q]
                low[l][k] = v * inv_diag[k]

        def solve(rows):
            out = []
            for l in range(b):
                v = rows[l]
                for q in range(l):
                    v = v - low[l][q] * out[q]
                out.append(v * inv_diag[l])
            return out

        def solve_back(rows):
            out = [None] * b
            for l in reversed(range(b)):
                v = rows[l]
                for q in range(l + 1, b):
                    v = v - low[q][l] * out[q]
                out[l] = v * inv_diag[l]
            return out

        x = solve(rows_m)
        store_rows(j0, x)
        if j0 + b == TILE:
            break
        va, vm = solve_back(solve(rows_a)), solve_back(x)
        drop = (j0 + b) // sub * sub - done
        if drop:
            a, m, done = a[drop:], m[drop:], done + drop
        height = TILE - done
        da = dm = None
        for k in range(b):
            col = jnp.broadcast_to(a[:, j0 + k : j0 + k + 1], (height, TILE))
            if done < j0 + b:
                col = jnp.where(line[:height] >= j0 + b - done, col, 0.0)
            ta = col * jnp.broadcast_to(va[k][0:1], (height, TILE))
            tm = col * jnp.broadcast_to(vm[k][0:1], (height, TILE))
            da, dm = (ta, tm) if k == 0 else (da + ta, dm + tm)
        a, m = a - da, m - dm


def split(x):
    high = x.astype(jnp.bfloat16)
    return high, (x - high.astype(jnp.float32)).astype(jnp.bfloat16)


def mul(x, y, transposed=False):
    dims = (((1,), (1 if transposed else 0,)), ((), ()))
    return lax.dot_general(x, y, dims, preferred_element_type=jnp.float32)


def mul3(x, y, transposed=False):
    xh, xl = split(x)
    yh, yl = split(y)
    return mul(xh, yh, transposed) + (mul(xh, yl, transposed) + mul(xl, yh, transposed))


def factor_leading(lead, work, inverse, lower, block_inv, inv_high, inv_low):
    width = WIDTH
    work[...] = lead[...].astype(jnp.float32)
    row_of = lax.broadcasted_iota(jnp.int32, (width, width), 0)
    col_of = lax.broadcasted_iota(jnp.int32, (width, width), 1)
    inverse[...] = jnp.where(row_of == col_of, 1.0, 0.0).astype(jnp.float32)

    def store_rows(j0, x):
        for k in range(len(x)):
            block_inv[j0 + k : j0 + k + 1, :] = x[k][0:1, :]

    def step(kb, _):
        o = pl.multiple_of(kb * TILE, TILE)
        here = pl.ds(o, TILE)
        invert_block(work[here, here], store_rows)
        d_inv = block_inv[...]
        below = mul3(work[:, here], d_inv, True)
        line = lax.broadcasted_iota(jnp.int32, (width, TILE), 0)
        lane = lax.broadcasted_iota(jnp.int32, (width, TILE), 1)
        lower[:, here] = jnp.where(line >= lane + o, below, 0.0)
        below = jnp.where(line >= o + TILE, below, 0.0)
        x_rows = mul3(d_inv, inverse[here, :])
        inverse[here, :] = x_rows
        work[...] = work[...] - mul3(below, below, True)
        inverse[...] = inverse[...] - mul3(below, x_rows)
        return 0

    lax.fori_loop(0, PANEL, step, 0)
    high, low = split(inverse[...])
    inv_high[...] = high
    inv_low[...] = low


def update_kernel(inv_high, inv_low, lower, top, panel, front, out, right):
    row_id = lax.axis_index("row")
    block_id = lax.axis_index("sub") * lax.axis_size("col") + lax.axis_index("col")
    tops = top[...]
    right[...] = mul(inv_high[...], tops) + mul(inv_low[...], tops)
    chunk = 128

    @pl.loop(0, panel.shape[0] // chunk)
    def _(t):
        rows = pl.ds(pl.multiple_of(t * chunk, chunk), chunk)
        a_rows = panel[rows, :]
        f_rows = mul(a_rows, inv_high[...], True) + mul(a_rows, inv_low[...], True)
        head = (row_id == 0) & (t < WIDTH // chunk)

        @pl.when(block_id == 0)
        def _():
            out[rows, :] = f_rows

            @pl.when(head)
            def _():
                out[rows, :] = lower[rows, :]

        @pl.when(block_id != 0)
        def _():
            @pl.when(head)
            def _():
                out[rows, :] = front[rows, :]

            @pl.when(jnp.logical_not(head))
            def _():
                out[rows, :] = front[rows, :] - mul3(f_rows, right[...])


def apply_update(inv_high, inv_low, lower, top, panel, front):
    vmem = pl.BlockSpec(memory_space=pltpu.VMEM)
    return pl.pallas_call(
        update_kernel,
        out_shape=jax.ShapeDtypeStruct(front.shape, jnp.float32),
        in_specs=[vmem] * 6,
        out_specs=vmem,
        scratch_shapes=[pltpu.VMEM((WIDTH, WIDTH), jnp.float32)],
        name="apply_update",
    )(inv_high, inv_low, lower, top, panel, front)


def body(child_update, parent_front, tile_map):
    tile_len = TILE
    panel_tiles = PANEL
    sub_count = lax.axis_size("sub")
    row_count = lax.axis_size("row")
    col_count = lax.axis_size("col")
    sub_id = lax.axis_index("sub")
    row_id = lax.axis_index("row")
    col_id = lax.axis_index("col")
    child_rows = child_update.shape[0] // tile_len
    child_cols = child_update.shape[1] // tile_len
    front_rows = parent_front.shape[0] // tile_len
    own_map = lax.dynamic_index_in_dim(tile_map, sub_id, 0, keepdims=False)
    own_cols = lax.dynamic_index_in_dim(
        own_map.reshape(child_cols, col_count), col_id, 1, keepdims=False
    )
    live_cols = own_cols >= 0
    destination = jnp.floor_divide(jnp.floor_divide(own_cols, panel_tiles), col_count)
    slot_index = jnp.remainder(own_cols, panel_tiles)
    dest_hit = destination[None, :] == jnp.arange(sub_count, dtype=jnp.int32)[:, None]
    slot_hit = slot_index[None, :] == jnp.arange(panel_tiles, dtype=jnp.int32)[:, None]
    select = (live_cols[None, None, :] & dest_hit[:, None, :] & slot_hit[None, :, :]).astype(
        jnp.bfloat16
    )
    column_slabs = child_update.reshape(child_rows * tile_len, child_cols, tile_len)
    payload = jnp.einsum(
        "dqk,rky->dqry", select, column_slabs, preferred_element_type=jnp.float32
    ).astype(jnp.bfloat16)
    maps_rows = lax.dynamic_index_in_dim(
        tile_map.reshape(sub_count, child_rows, row_count), row_id, 2, keepdims=False
    )
    local_row = jnp.floor_divide(
        jnp.floor_divide(maps_rows, panel_tiles), row_count
    ) * panel_tiles + jnp.remainder(maps_rows, panel_tiles)
    row_hit = (maps_rows[:, :, None] >= 0) & (
        local_row[:, :, None] == jnp.arange(front_rows, dtype=jnp.int32)[None, None, :]
    )
    place_row = row_hit.astype(jnp.bfloat16)
    arrived = lax.all_to_all(payload, "sub", split_axis=0, concat_axis=0, tiled=True)
    slot_count = arrived.shape[1]
    grid = arrived.reshape(sub_count, slot_count, child_rows, tile_len, tile_len)
    spread = jnp.einsum("ska,sqkyx->ayqx", place_row, grid, preferred_element_type=jnp.float32)
    placed = spread.reshape(front_rows * tile_len, slot_count * tile_len)
    front_local = parent_front.astype(jnp.float32) + placed
    panel, top, inv_high, inv_low, lower = spread_panels(
        front_local.astype(jnp.bfloat16), sub_count, row_count, col_count
    )
    return apply_update(inv_high, inv_low, lower, top, panel, front_local)


def solution(mesh):
    in_specs = (P(("sub", "row"), "col"), P("row", ("sub", "col")), P())
    out_specs = P("row", ("sub", "col"))
    return jax.shard_map(body, mesh=mesh, in_specs=in_specs, out_specs=out_specs, check_vma=False)
```

```python
import functools

import jax
import jax.numpy as jnp
from jax import lax
from jax.experimental import pallas as pl
from jax.experimental.pallas import tpu as pltpu
from jax.sharding import PartitionSpec as P

TILE = 128
PANEL = 4
WIDTH = TILE * PANEL
MESH = pl.DeviceIdType.MESH
GROUP = 8
PIECE = WIDTH // GROUP


def remote(src, dst, send_sem, recv_sem, device):
    return pltpu.make_async_remote_copy(
        src_ref=src,
        dst_ref=dst,
        send_sem=send_sem,
        recv_sem=recv_sem,
        device_id=device,
        device_id_type=MESH,
    )


def each(count, skip, fn):
    def step(i, _):
        @pl.when(i != skip)
        def _():
            fn(i)

        return 0

    lax.fori_loop(0, count, step, 0)


def spread_kernel(
    n_sub,
    n_row,
    n_col,
    front,
    panel,
    top,
    inv_high,
    inv_low,
    lower,
    lead,
    work,
    inverse,
    block_inv,
    local_sem,
    top_send,
    top_cross,
    top_gather,
    top_recv,
    panel_col,
    panel_sub,
    panel_recv,
    panel_far,
    ring_right,
    ring_left,
    lead_sub,
    lead_col,
    lead_gather,
    lead_recv,
):
    s, r, c = lax.axis_index("sub"), lax.axis_index("row"), lax.axis_index("col")
    p = s * n_col + c
    half, i = r // GROUP, r % GROUP
    depth = front.shape[0] // n_col

    def at_group(j):
        return (s, half * GROUP + j, c)

    def top_piece(j):
        return top.at[pl.ds(pl.multiple_of(j * PIECE, PIECE), PIECE)]

    def lead_piece(j):
        return lead.at[pl.ds(pl.multiple_of(j * PIECE, PIECE), PIECE)]

    def panel_piece(q):
        return panel.at[pl.ds(pl.multiple_of(q * depth, depth), depth)]

    def front_piece(q):
        return front.at[pl.ds(pl.multiple_of(q * depth, depth), depth)]

    def front_top(j):
        return front.at[pl.ds(pl.multiple_of(j * PIECE, PIECE), PIECE)]

    barrier = pltpu.get_barrier_semaphore()
    across = (s, (1 - half) * GROUP + i, c)

    def greet(device):
        pl.semaphore_signal(barrier, inc=1, device_id=device, device_id_type=MESH)

    each(n_sub, s, lambda k: greet((k, r, c)))
    each(n_col, c, lambda k: greet((s, r, k)))
    each(GROUP, i, lambda j: greet(at_group(j)))
    greet(across)
    pl.semaphore_wait(barrier, n_sub - 1 + n_col - 1 + GROUP - 1 + 1)

    top_scatter = lambda j: remote(
        front_top(j), top_piece(j), top_send.at[j], top_recv.at[j], at_group(j)
    )
    panel_along = lambda k: remote(
        front_piece(k), panel_piece(k), panel_col.at[k], panel_recv.at[k], (0, r, k)
    )
    root_down = lambda k: remote(
        front_piece(0), panel_piece(0), panel_sub.at[k], panel_recv.at[0], (k, r, 0)
    )
    panel_down = lambda k: remote(
        panel_piece(c), panel_piece(c), panel_sub.at[k], panel_recv.at[c], (k, r, c)
    )
    right, left = (c + 1) % n_col, (c + n_col - 1) % n_col
    last = n_col // 2

    def from_left(t):
        return (c + n_col - t) % n_col

    def from_right(t):
        return (c + t) % n_col

    def ring_copies(t):
        go_right, go_left = panel_piece(from_left(t - 1)), panel_piece(from_right(t - 1))
        left_sem = panel_recv.at[from_right(t - 1)]
        if t == last:
            go_right = go_right.at[pl.ds(0, depth // 2)]
            go_left = go_left.at[pl.ds(depth // 2, depth // 2)]
            left_sem = panel_far
        return (
            remote(
                go_right, go_right, ring_right.at[t], panel_recv.at[from_left(t - 1)], (s, r, right)
            ),
            remote(go_left, go_left, ring_left.at[t], left_sem, (s, r, left)),
        )

    to_right, to_left = (s != 0) | (right != 0), (s != 0) | (left != 0)

    def ring_step(t):
        @pl.when((p != 0) & ((t > 1) | (s != 0)))
        def _():
            arrived(panel_piece(from_left(t - 1)), panel_recv.at[from_left(t - 1)])
            if t > 1:
                arrived(panel_piece(from_right(t - 1)), panel_recv.at[from_right(t - 1)])

        go_right, go_left = ring_copies(t)
        pl.when(to_right)(go_right.start)
        pl.when(to_left)(go_left.start)

    top_over = remote(top_piece(i), top_piece(i), top_cross, top_recv.at[i], across)
    top_share = lambda j: remote(
        top_piece(i), top_piece(i), top_gather.at[j], top_recv.at[i], at_group(j)
    )
    lead_down = lambda k: remote(
        top_piece(i), lead_piece(i), lead_sub.at[k], lead_recv.at[i], (k, r, 0)
    )
    lead_along = lambda k: remote(
        top_piece(i), lead_piece(i), lead_col.at[k], lead_recv.at[i], (s, r, k)
    )
    lead_forward = lambda k: remote(
        lead_piece(i), lead_piece(i), lead_col.at[k], lead_recv.at[i], (s, r, k)
    )
    lead_share = lambda j: remote(
        lead_piece(i), lead_piece(i), lead_gather.at[j], lead_recv.at[i], at_group(j)
    )
    own_top = pltpu.make_async_copy(front.at[pl.ds(0, WIDTH)], top, local_sem.at[0])
    own_panel = pltpu.make_async_copy(front, panel, local_sem.at[1])
    own_lead = pltpu.make_async_copy(top, lead, local_sem.at[2])

    def arrived(piece, sem):
        pltpu.make_async_copy(piece, piece, sem).wait()

    def share_top():
        each(GROUP, i, lambda j: pl.when((j != 0) | (half != 0))(lambda: top_share(j).start()))

    @pl.when(r == 0)
    def _():
        own_top.start()
        each(GROUP, 0, lambda j: top_scatter(j).start())
        own_top.wait()

    @pl.when((r != 0) & (half == 0))
    def _():
        arrived(top_piece(i), top_recv.at[i])

    @pl.when(half == 0)
    def _():
        top_over.start()

    @pl.when(p == 0)
    def _():
        @pl.when(half != 0)
        def _():
            arrived(top_piece(i), top_recv.at[i])

        each(n_sub, 0, lambda k: lead_down(k).start())
        each(n_col, 0, lambda k: lead_along(k).start())
        own_panel.start()
        each(n_sub, 0, lambda k: root_down(k).start())
        for k in sorted(range(1, n_col), key=lambda k: -min(k, n_col - k)):
            panel_along(k).start()
        share_top()
        own_panel.wait()

    @pl.when(p != 0)
    def _():
        arrived(lead_piece(i), lead_recv.at[i])

        @pl.when(c == 0)
        def _():
            each(n_col, 0, lambda k: lead_forward(k).start())

        each(GROUP, i, lambda j: lead_share(j).start())

        @pl.when(half != 0)
        def _():
            arrived(top_piece(i), top_recv.at[i])

        share_top()

        @pl.when(s == 0)
        def _():
            arrived(panel_piece(c), panel_recv.at[c])
            each(n_sub, 0, lambda k: panel_down(k).start())

    def all_of_top():
        each(GROUP, i, lambda j: arrived(top_piece(j), top_recv.at[j]))

    pl.when((r != 0) & (p == 0))(all_of_top)

    @pl.when(p == 0)
    def _():
        own_lead.start()
        own_lead.wait()

    @pl.when(p != 0)
    def _():
        each(GROUP, i, lambda j: arrived(lead_piece(j), lead_recv.at[j]))

    def between(kb):
        for t in range(1, last):
            pl.when(kb == t)(functools.partial(ring_step, t))

    factor_leading(lead, work, inverse, lower, block_inv, inv_high, inv_low, between)
    ring_step(last)

    pl.when((r != 0) & (p != 0))(all_of_top)

    @pl.when(p != 0)
    def _():
        low = panel_piece(from_left(last)).at[pl.ds(0, depth // 2)]
        high = panel_piece(from_left(last)).at[pl.ds(depth // 2, depth // 2)]
        arrived(low, panel_recv.at[from_left(last)])
        arrived(high, panel_far)

    @pl.when(r == 0)
    def _():
        each(GROUP, 0, lambda j: top_scatter(j).wait_send())

    @pl.when(half == 0)
    def _():
        top_over.wait_send()
        each(GROUP, i, lambda j: pl.when(j != 0)(lambda: top_share(j).wait_send()))

    @pl.when(half != 0)
    def _():
        each(GROUP, i, lambda j: top_share(j).wait_send())

    @pl.when(p == 0)
    def _():
        each(n_sub, 0, lambda k: root_down(k).wait_send())
        each(n_col, 0, lambda k: panel_along(k).wait_send())
        each(n_sub, 0, lambda k: lead_down(k).wait_send())
        each(n_col, 0, lambda k: lead_along(k).wait_send())

    @pl.when(p != 0)
    def _():
        @pl.when(s == 0)
        def _():
            each(n_sub, 0, lambda k: panel_down(k).wait_send())

        @pl.when(c == 0)
        def _():
            each(n_col, 0, lambda k: lead_forward(k).wait_send())

        each(GROUP, i, lambda j: lead_share(j).wait_send())

    for t in range(1, last + 1):
        go_right, go_left = ring_copies(t)
        pl.when(to_right)(go_right.wait_send)
        pl.when(to_left)(go_left.wait_send)


def spread_panels(front16, n_sub, n_row, n_col):
    rows, width = front16.shape
    vmem = pl.BlockSpec(memory_space=pltpu.VMEM)
    dma = pltpu.SemaphoreType.DMA
    return pl.pallas_call(
        functools.partial(spread_kernel, n_sub, n_row, n_col),
        out_shape=(
            jax.ShapeDtypeStruct((rows, width), jnp.bfloat16),
            jax.ShapeDtypeStruct((WIDTH, width), jnp.bfloat16),
            jax.ShapeDtypeStruct((WIDTH, WIDTH), jnp.bfloat16),
            jax.ShapeDtypeStruct((WIDTH, WIDTH), jnp.bfloat16),
            jax.ShapeDtypeStruct((WIDTH, WIDTH), jnp.float32),
        ),
        in_specs=[vmem],
        out_specs=(vmem,) * 5,
        scratch_shapes=[
            pltpu.VMEM((WIDTH, WIDTH), jnp.bfloat16),
            pltpu.VMEM((WIDTH, WIDTH), jnp.float32),
            pltpu.VMEM((WIDTH, WIDTH), jnp.float32),
            pltpu.VMEM((TILE, TILE), jnp.float32),
            dma((3,)),
            dma((GROUP,)),
            dma(()),
            dma((GROUP,)),
            dma((GROUP,)),
            dma((n_col,)),
            dma((n_sub,)),
            dma((n_col,)),
            dma(()),
            dma((n_col,)),
            dma((n_col,)),
            dma((n_sub,)),
            dma((n_col,)),
            dma((GROUP,)),
            dma((GROUP,)),
        ],
        compiler_params=pltpu.CompilerParams(collective_id=0, has_side_effects=True),
        name="spread_panels",
    )(front16)


def invert_block(block, store_rows):
    sub = 8
    b = 4
    line = lax.broadcasted_iota(jnp.int32, (TILE, TILE), 0)
    lane = lax.broadcasted_iota(jnp.int32, (TILE, TILE), 1)
    a = block
    m = jnp.where(lane == line, 1.0, 0.0).astype(jnp.float32)
    done = 0
    for j0 in range(0, TILE, b):
        i0 = j0 - done
        rows_a = [jnp.broadcast_to(a[i0 + k : i0 + k + 1, :], (sub, TILE)) for k in range(b)]
        rows_m = [jnp.broadcast_to(m[i0 + k : i0 + k + 1, :], (sub, TILE)) for k in range(b)]
        piv = [
            [
                jnp.broadcast_to(rows_a[l][:, j0 + k : j0 + k + 1], (sub, TILE))
                for k in range(l + 1)
            ]
            for l in range(b)
        ]
        low = [[None] * b for _ in range(b)]
        inv_diag = [None] * b
        for k in range(b):
            d = piv[k][k]
            for q in range(k):
                d = d - low[k][q] * low[k][q]
            inv_diag[k] = lax.rsqrt(d)
            for l in range(k + 1, b):
                v = piv[l][k]
                for q in range(k):
                    v = v - low[l][q] * low[k][q]
                low[l][k] = v * inv_diag[k]

        def solve(rows):
            out = []
            for l in range(b):
                v = rows[l]
                for q in range(l):
                    v = v - low[l][q] * out[q]
                out.append(v * inv_diag[l])
            return out

        def solve_back(rows):
            out = [None] * b
            for l in reversed(range(b)):
                v = rows[l]
                for q in range(l + 1, b):
                    v = v - low[q][l] * out[q]
                out[l] = v * inv_diag[l]
            return out

        x = solve(rows_m)
        store_rows(j0, x)
        if j0 + b == TILE:
            break
        va, vm = solve_back(solve(rows_a)), solve_back(x)
        drop = (j0 + b) // sub * sub - done
        if drop:
            a, m, done = a[drop:], m[drop:], done + drop
        height = TILE - done
        da = dm = None
        for k in range(b):
            col = jnp.broadcast_to(a[:, j0 + k : j0 + k + 1], (height, TILE))
            if done < j0 + b:
                col = jnp.where(line[:height] >= j0 + b - done, col, 0.0)
            ta = col * jnp.broadcast_to(va[k][0:1], (height, TILE))
            tm = col * jnp.broadcast_to(vm[k][0:1], (height, TILE))
            da, dm = (ta, tm) if k == 0 else (da + ta, dm + tm)
        a, m = a - da, m - dm


def split(x):
    high = x.astype(jnp.bfloat16)
    return high, (x - high.astype(jnp.float32)).astype(jnp.bfloat16)


def mul(x, y, transposed=False):
    dims = (((1,), (1 if transposed else 0,)), ((), ()))
    return lax.dot_general(x, y, dims, preferred_element_type=jnp.float32)


def mul3(x, y, transposed=False):
    xh, xl = split(x)
    yh, yl = split(y)
    return mul(xh, yh, transposed) + (mul(xh, yl, transposed) + mul(xl, yh, transposed))


def factor_leading(lead, work, inverse, lower, block_inv, inv_high, inv_low, between):
    width = WIDTH
    work[...] = lead[...].astype(jnp.float32)
    row_of = lax.broadcasted_iota(jnp.int32, (width, width), 0)
    col_of = lax.broadcasted_iota(jnp.int32, (width, width), 1)
    inverse[...] = jnp.where(row_of == col_of, 1.0, 0.0).astype(jnp.float32)

    def store_rows(j0, x):
        for k in range(len(x)):
            block_inv[j0 + k : j0 + k + 1, :] = x[k][0:1, :]

    def step(kb, _):
        between(kb)
        o = pl.multiple_of(kb * TILE, TILE)
        here = pl.ds(o, TILE)
        invert_block(work[here, here], store_rows)
        d_inv = block_inv[...]
        below = mul3(work[:, here], d_inv, True)
        line = lax.broadcasted_iota(jnp.int32, (width, TILE), 0)
        lane = lax.broadcasted_iota(jnp.int32, (width, TILE), 1)
        lower[:, here] = jnp.where(line >= lane + o, below, 0.0)
        below = jnp.where(line >= o + TILE, below, 0.0)
        x_rows = mul3(d_inv, inverse[here, :])
        inverse[here, :] = x_rows
        work[...] = work[...] - mul3(below, below, True)
        inverse[...] = inverse[...] - mul3(below, x_rows)
        return 0

    lax.fori_loop(0, PANEL, step, 0)
    high, low = split(inverse[...])
    inv_high[...] = high
    inv_low[...] = low


def update_kernel(inv_high, inv_low, lower, top, panel, front, out, right):
    row_id = lax.axis_index("row")
    block_id = lax.axis_index("sub") * lax.axis_size("col") + lax.axis_index("col")
    tops = top[...]
    right[...] = mul(inv_high[...], tops) + mul(inv_low[...], tops)
    chunk = 128

    @pl.loop(0, panel.shape[0] // chunk)
    def _(t):
        rows = pl.ds(pl.multiple_of(t * chunk, chunk), chunk)
        a_rows = panel[rows, :]
        f_rows = mul(a_rows, inv_high[...], True) + mul(a_rows, inv_low[...], True)
        head = (row_id == 0) & (t < WIDTH // chunk)

        @pl.when(block_id == 0)
        def _():
            out[rows, :] = f_rows

            @pl.when(head)
            def _():
                out[rows, :] = lower[rows, :]

        @pl.when(block_id != 0)
        def _():
            @pl.when(head)
            def _():
                out[rows, :] = front[rows, :]

            @pl.when(jnp.logical_not(head))
            def _():
                out[rows, :] = front[rows, :] - mul3(f_rows, right[...])


def apply_update(inv_high, inv_low, lower, top, panel, front):
    vmem = pl.BlockSpec(memory_space=pltpu.VMEM)
    return pl.pallas_call(
        update_kernel,
        out_shape=jax.ShapeDtypeStruct(front.shape, jnp.float32),
        in_specs=[vmem] * 6,
        out_specs=vmem,
        scratch_shapes=[pltpu.VMEM((WIDTH, WIDTH), jnp.float32)],
        name="apply_update",
    )(inv_high, inv_low, lower, top, panel, front)


def body(child_update, parent_front, tile_map):
    tile_len = TILE
    panel_tiles = PANEL
    sub_count = lax.axis_size("sub")
    row_count = lax.axis_size("row")
    col_count = lax.axis_size("col")
    sub_id = lax.axis_index("sub")
    row_id = lax.axis_index("row")
    col_id = lax.axis_index("col")
    child_rows = child_update.shape[0] // tile_len
    child_cols = child_update.shape[1] // tile_len
    front_rows = parent_front.shape[0] // tile_len
    own_map = lax.dynamic_index_in_dim(tile_map, sub_id, 0, keepdims=False)
    own_cols = lax.dynamic_index_in_dim(
        own_map.reshape(child_cols, col_count), col_id, 1, keepdims=False
    )
    live_cols = own_cols >= 0
    destination = jnp.floor_divide(jnp.floor_divide(own_cols, panel_tiles), col_count)
    slot_index = jnp.remainder(own_cols, panel_tiles)
    dest_hit = destination[None, :] == jnp.arange(sub_count, dtype=jnp.int32)[:, None]
    slot_hit = slot_index[None, :] == jnp.arange(panel_tiles, dtype=jnp.int32)[:, None]
    select = (live_cols[None, None, :] & dest_hit[:, None, :] & slot_hit[None, :, :]).astype(
        jnp.bfloat16
    )
    column_slabs = child_update.reshape(child_rows * tile_len, child_cols, tile_len)
    payload = jnp.einsum(
        "dqk,rky->dqry", select, column_slabs, preferred_element_type=jnp.float32
    ).astype(jnp.bfloat16)
    maps_rows = lax.dynamic_index_in_dim(
        tile_map.reshape(sub_count, child_rows, row_count), row_id, 2, keepdims=False
    )
    local_row = jnp.floor_divide(
        jnp.floor_divide(maps_rows, panel_tiles), row_count
    ) * panel_tiles + jnp.remainder(maps_rows, panel_tiles)
    row_hit = (maps_rows[:, :, None] >= 0) & (
        local_row[:, :, None] == jnp.arange(front_rows, dtype=jnp.int32)[None, None, :]
    )
    place_row = row_hit.astype(jnp.bfloat16)
    arrived = lax.all_to_all(payload, "sub", split_axis=0, concat_axis=0, tiled=True)
    slot_count = arrived.shape[1]
    grid = arrived.reshape(sub_count, slot_count, child_rows, tile_len, tile_len)
    spread = jnp.einsum("ska,sqkyx->ayqx", place_row, grid, preferred_element_type=jnp.float32)
    placed = spread.reshape(front_rows * tile_len, slot_count * tile_len)
    front_local = parent_front.astype(jnp.float32) + placed
    panel, top, inv_high, inv_low, lower = spread_panels(
        front_local.astype(jnp.bfloat16), sub_count, row_count, col_count
    )
    return apply_update(inv_high, inv_low, lower, top, panel, front_local)


def solution(mesh):
    in_specs = (P(("sub", "row"), "col"), P("row", ("sub", "col")), P())
    out_specs = P("row", ("sub", "col"))
    return jax.shard_map(body, mesh=mesh, in_specs=in_specs, out_specs=out_specs, check_vma=False)
```

```python
import functools

import jax
import jax.numpy as jnp
from jax import lax
from jax.experimental import pallas as pl
from jax.experimental.pallas import tpu as pltpu
from jax.sharding import PartitionSpec as P

TILE = 128
PANEL = 4
WIDTH = TILE * PANEL
MESH = pl.DeviceIdType.MESH
GROUP = 8
PIECE = WIDTH // GROUP


def remote(src, dst, send_sem, recv_sem, device):
    return pltpu.make_async_remote_copy(
        src_ref=src,
        dst_ref=dst,
        send_sem=send_sem,
        recv_sem=recv_sem,
        device_id=device,
        device_id_type=MESH,
    )


def each(count, skip, fn):
    def step(i, _):
        @pl.when(i != skip)
        def _():
            fn(i)

        return 0

    lax.fori_loop(0, count, step, 0)


def spread_kernel(
    n_sub,
    n_row,
    n_col,
    front,
    lead,
    panel,
    top,
    inv_high,
    inv_low,
    lower,
    work,
    inverse,
    block_inv,
    local_sem,
    top_send,
    top_cross,
    top_gather,
    top_recv,
    panel_col,
    panel_sub,
    panel_recv,
    panel_far,
    ring_right,
    ring_left,
):
    s, r, c = lax.axis_index("sub"), lax.axis_index("row"), lax.axis_index("col")
    p = s * n_col + c
    half, i = r // GROUP, r % GROUP
    depth = front.shape[0] // n_col

    def at_group(j):
        return (s, half * GROUP + j, c)

    def top_piece(j):
        return top.at[pl.ds(pl.multiple_of(j * PIECE, PIECE), PIECE)]

    def panel_piece(q):
        return panel.at[pl.ds(pl.multiple_of(q * depth, depth), depth)]

    def front_piece(q):
        return front.at[pl.ds(pl.multiple_of(q * depth, depth), depth)]

    def front_top(j):
        return front.at[pl.ds(pl.multiple_of(j * PIECE, PIECE), PIECE)]

    barrier = pltpu.get_barrier_semaphore()
    across = (s, (1 - half) * GROUP + i, c)

    def greet(device):
        pl.semaphore_signal(barrier, inc=1, device_id=device, device_id_type=MESH)

    each(n_sub, s, lambda k: greet((k, r, c)))
    each(n_col, c, lambda k: greet((s, r, k)))
    each(GROUP, i, lambda j: greet(at_group(j)))
    greet(across)
    pl.semaphore_wait(barrier, n_sub - 1 + n_col - 1 + GROUP - 1 + 1)

    top_scatter = lambda j: remote(
        front_top(j), top_piece(j), top_send.at[j], top_recv.at[j], at_group(j)
    )
    panel_along = lambda k: remote(
        front_piece(k), panel_piece(k), panel_col.at[k], panel_recv.at[k], (0, r, k)
    )
    root_down = lambda k: remote(
        front_piece(0), panel_piece(0), panel_sub.at[k], panel_recv.at[0], (k, r, 0)
    )
    panel_down = lambda k: remote(
        panel_piece(c), panel_piece(c), panel_sub.at[k], panel_recv.at[c], (k, r, c)
    )
    right, left = (c + 1) % n_col, (c + n_col - 1) % n_col
    last = n_col // 2

    def from_left(t):
        return (c + n_col - t) % n_col

    def from_right(t):
        return (c + t) % n_col

    def ring_copies(t):
        go_right, go_left = panel_piece(from_left(t - 1)), panel_piece(from_right(t - 1))
        left_sem = panel_recv.at[from_right(t - 1)]
        if t == last:
            go_right = go_right.at[pl.ds(0, depth // 2)]
            go_left = go_left.at[pl.ds(depth // 2, depth // 2)]
            left_sem = panel_far
        return (
            remote(
                go_right, go_right, ring_right.at[t], panel_recv.at[from_left(t - 1)], (s, r, right)
            ),
            remote(go_left, go_left, ring_left.at[t], left_sem, (s, r, left)),
        )

    to_right, to_left = (s != 0) | (right != 0), (s != 0) | (left != 0)

    def ring_step(t):
        @pl.when((p != 0) & ((t > 1) | (s != 0)))
        def _():
            arrived(panel_piece(from_left(t - 1)), panel_recv.at[from_left(t - 1)])
            if t > 1:
                arrived(panel_piece(from_right(t - 1)), panel_recv.at[from_right(t - 1)])

        go_right, go_left = ring_copies(t)
        pl.when(to_right)(go_right.start)
        pl.when(to_left)(go_left.start)

    top_over = remote(top_piece(i), top_piece(i), top_cross, top_recv.at[i], across)
    top_share = lambda j: remote(
        top_piece(i), top_piece(i), top_gather.at[j], top_recv.at[i], at_group(j)
    )
    own_top = pltpu.make_async_copy(front.at[pl.ds(0, WIDTH)], top, local_sem.at[0])
    own_panel = pltpu.make_async_copy(front, panel, local_sem.at[1])

    def arrived(piece, sem):
        pltpu.make_async_copy(piece, piece, sem).wait()

    def share_top():
        each(GROUP, i, lambda j: pl.when((j != 0) | (half != 0))(lambda: top_share(j).start()))

    @pl.when(r == 0)
    def _():
        own_top.start()
        each(GROUP, 0, lambda j: top_scatter(j).start())
        own_top.wait()

    @pl.when((r != 0) & (half == 0))
    def _():
        arrived(top_piece(i), top_recv.at[i])

    @pl.when(half == 0)
    def _():
        top_over.start()

    @pl.when(p == 0)
    def _():
        own_panel.start()
        each(n_sub, 0, lambda k: root_down(k).start())
        for k in sorted(range(1, n_col), key=lambda k: -min(k, n_col - k)):
            panel_along(k).start()
        own_panel.wait()

    pl.when(half == 0)(share_top)

    def pass_down():
        @pl.when((s == 0) & (c != 0))
        def _():
            arrived(panel_piece(c), panel_recv.at[c])
            each(n_sub, 0, lambda k: panel_down(k).start())

        @pl.when(half != 0)
        def _():
            arrived(top_piece(i), top_recv.at[i])
            share_top()

    def between(kb):
        pl.when(kb == 1)(pass_down)
        for t in range(1, last - 1):
            pl.when(kb == t + 1)(functools.partial(ring_step, t))

    factor_leading(lead, work, inverse, lower, block_inv, inv_high, inv_low, between)
    ring_step(last - 1)
    ring_step(last)

    @pl.when(r != 0)
    def _():
        each(GROUP, i, lambda j: arrived(top_piece(j), top_recv.at[j]))

    @pl.when(p != 0)
    def _():
        low = panel_piece(from_left(last)).at[pl.ds(0, depth // 2)]
        high = panel_piece(from_left(last)).at[pl.ds(depth // 2, depth // 2)]
        arrived(low, panel_recv.at[from_left(last)])
        arrived(high, panel_far)

    @pl.when(r == 0)
    def _():
        each(GROUP, 0, lambda j: top_scatter(j).wait_send())

    @pl.when(half == 0)
    def _():
        top_over.wait_send()
        each(GROUP, i, lambda j: pl.when(j != 0)(lambda: top_share(j).wait_send()))

    @pl.when(half != 0)
    def _():
        each(GROUP, i, lambda j: top_share(j).wait_send())

    @pl.when(p == 0)
    def _():
        each(n_sub, 0, lambda k: root_down(k).wait_send())
        each(n_col, 0, lambda k: panel_along(k).wait_send())

    @pl.when((p != 0) & (s == 0))
    def _():
        each(n_sub, 0, lambda k: panel_down(k).wait_send())

    for t in range(1, last + 1):
        go_right, go_left = ring_copies(t)
        pl.when(to_right)(go_right.wait_send)
        pl.when(to_left)(go_left.wait_send)


def spread_panels(front16, lead, n_sub, n_row, n_col):
    rows, width = front16.shape
    vmem = pl.BlockSpec(memory_space=pltpu.VMEM)
    dma = pltpu.SemaphoreType.DMA
    return pl.pallas_call(
        functools.partial(spread_kernel, n_sub, n_row, n_col),
        out_shape=(
            jax.ShapeDtypeStruct((rows, width), jnp.bfloat16),
            jax.ShapeDtypeStruct((WIDTH, width), jnp.bfloat16),
            jax.ShapeDtypeStruct((WIDTH, WIDTH), jnp.bfloat16),
            jax.ShapeDtypeStruct((WIDTH, WIDTH), jnp.bfloat16),
            jax.ShapeDtypeStruct((WIDTH, WIDTH), jnp.float32),
        ),
        in_specs=[vmem, vmem],
        out_specs=(vmem,) * 5,
        scratch_shapes=[
            pltpu.VMEM((WIDTH, WIDTH), jnp.float32),
            pltpu.VMEM((WIDTH, WIDTH), jnp.float32),
            pltpu.VMEM((TILE, TILE), jnp.float32),
            dma((2,)),
            dma((GROUP,)),
            dma(()),
            dma((GROUP,)),
            dma((GROUP,)),
            dma((n_col,)),
            dma((n_sub,)),
            dma((n_col,)),
            dma(()),
            dma((n_col,)),
            dma((n_col,)),
        ],
        compiler_params=pltpu.CompilerParams(collective_id=0, has_side_effects=True),
        name="spread_panels",
    )(front16, lead)


def lead_kernel(
    n_sub,
    n_row,
    n_col,
    contribution,
    parent,
    lead,
    raw,
    local_sem,
    raw_send,
    parent_send,
    cross_send,
    parent_cross,
    raw_recv,
    half_send,
    col_send,
    share_send,
    lead_recv,
):
    s, r, c = lax.axis_index("sub"), lax.axis_index("row"), lax.axis_index("col")
    half, i = r // GROUP, r % GROUP
    across = (s, (1 - half) * GROUP + i, c)

    def at_group(j):
        return (s, half * GROUP + j, c)

    def rows_of(ref, j):
        return ref.at[pl.ds(pl.multiple_of(j * PIECE, PIECE), PIECE)]

    barrier = pltpu.get_barrier_semaphore()

    def greet(device):
        pl.semaphore_signal(barrier, inc=1, device_id=device, device_id_type=MESH)

    each(n_sub, s, lambda k: greet((k, r, c)))
    each(n_col, c, lambda k: greet((s, r, k)))
    each(GROUP, i, lambda j: greet(at_group(j)))
    greet(across)
    pl.semaphore_wait(barrier, n_sub - 1 + n_col - 1 + GROUP - 1 + 1)

    def arrived(piece, sem):
        pltpu.make_async_copy(piece, piece, sem).wait()

    scatter = lambda j: remote(
        rows_of(contribution, j), raw.at[s], raw_send.at[j], raw_recv.at[s], at_group(j)
    )
    scatter_parent = lambda j: remote(
        rows_of(parent, j), raw.at[n_sub], parent_send.at[j], raw_recv.at[n_sub], at_group(j)
    )
    exchange = lambda k: remote(raw.at[s], raw.at[s], cross_send.at[k], raw_recv.at[s], (k, r, c))
    exchange_parent = lambda k: remote(
        raw.at[n_sub], raw.at[n_sub], parent_cross.at[k], raw_recv.at[n_sub], (k, r, c)
    )
    own = pltpu.make_async_copy(rows_of(contribution, 0), raw.at[s], local_sem.at[0])
    own_parent = pltpu.make_async_copy(rows_of(parent, 0), raw.at[n_sub], local_sem.at[1])
    mine = rows_of(lead, i)
    over = remote(mine, mine, half_send, lead_recv.at[i], across)
    along = lambda k: remote(mine, mine, col_send.at[k], lead_recv.at[i], (s, r, k))
    share = lambda j: remote(mine, mine, share_send.at[j], lead_recv.at[i], at_group(j))
    adds = (c == 0) & (half == 0)
    first = (c == 0) & (r == 0)

    @pl.when(first)
    def _():
        own.start()
        each(GROUP, 0, lambda j: scatter(j).start())

        @pl.when(s == 0)
        def _():
            own_parent.start()
            each(GROUP, 0, lambda j: scatter_parent(j).start())
            own_parent.wait()

        own.wait()

    @pl.when(adds & (r != 0))
    def _():
        arrived(raw.at[s], raw_recv.at[s])

        @pl.when(s == 0)
        def _():
            arrived(raw.at[n_sub], raw_recv.at[n_sub])

    @pl.when(adds)
    def _():
        each(n_sub, s, lambda k: exchange(k).start())

        @pl.when(s == 0)
        def _():
            each(n_sub, 0, lambda k: exchange_parent(k).start())

        each(n_sub, s, lambda k: arrived(raw.at[k], raw_recv.at[k]))

        @pl.when(s != 0)
        def _():
            arrived(raw.at[n_sub], raw_recv.at[n_sub])

        total = raw[n_sub].astype(jnp.float32)
        for k in range(n_sub):
            total = total + raw[k].astype(jnp.float32)
        lead[pl.ds(pl.multiple_of(i * PIECE, PIECE), PIECE), :] = total.astype(jnp.bfloat16)
        each(n_sub, s, lambda k: exchange(k).wait_send())

        @pl.when(s == 0)
        def _():
            each(n_sub, 0, lambda k: exchange_parent(k).wait_send())

        over.start()

    @pl.when(jnp.logical_not(adds))
    def _():
        arrived(mine, lead_recv.at[i])

    @pl.when(c == 0)
    def _():
        each(n_col, 0, lambda k: along(k).start())

    each(GROUP, i, lambda j: share(j).start())
    each(GROUP, i, lambda j: arrived(rows_of(lead, j), lead_recv.at[j]))

    @pl.when(first)
    def _():
        each(GROUP, 0, lambda j: scatter(j).wait_send())

        @pl.when(s == 0)
        def _():
            each(GROUP, 0, lambda j: scatter_parent(j).wait_send())

    pl.when(adds)(over.wait_send)

    @pl.when(c == 0)
    def _():
        each(n_col, 0, lambda k: along(k).wait_send())

    each(GROUP, i, lambda j: share(j).wait_send())


def spread_leading(contribution, parent, n_sub, n_row, n_col):
    vmem = pl.BlockSpec(memory_space=pltpu.VMEM)
    dma = pltpu.SemaphoreType.DMA
    return pl.pallas_call(
        functools.partial(lead_kernel, n_sub, n_row, n_col),
        out_shape=jax.ShapeDtypeStruct((WIDTH, WIDTH), jnp.bfloat16),
        in_specs=[vmem, vmem],
        out_specs=vmem,
        scratch_shapes=[
            pltpu.VMEM((n_sub + 1, PIECE, WIDTH), jnp.bfloat16),
            dma((2,)),
            dma((GROUP,)),
            dma((GROUP,)),
            dma((n_sub,)),
            dma((n_sub,)),
            dma((n_sub + 1,)),
            dma(()),
            dma((n_col,)),
            dma((GROUP,)),
            dma((GROUP,)),
        ],
        cost_estimate=pl.CostEstimate(flops=0, bytes_accessed=40_000_000, transcendentals=0),
        compiler_params=pltpu.CompilerParams(collective_id=1, has_side_effects=True),
        name="spread_leading",
    )(contribution, parent)


def invert_block(block, store_rows):
    sub = 8
    b = 4
    line = lax.broadcasted_iota(jnp.int32, (TILE, TILE), 0)
    lane = lax.broadcasted_iota(jnp.int32, (TILE, TILE), 1)
    a = block
    m = jnp.where(lane == line, 1.0, 0.0).astype(jnp.float32)
    done = 0
    for j0 in range(0, TILE, b):
        i0 = j0 - done
        rows_a = [jnp.broadcast_to(a[i0 + k : i0 + k + 1, :], (sub, TILE)) for k in range(b)]
        rows_m = [jnp.broadcast_to(m[i0 + k : i0 + k + 1, :], (sub, TILE)) for k in range(b)]
        piv = [
            [
                jnp.broadcast_to(rows_a[l][:, j0 + k : j0 + k + 1], (sub, TILE))
                for k in range(l + 1)
            ]
            for l in range(b)
        ]
        low = [[None] * b for _ in range(b)]
        inv_diag = [None] * b
        for k in range(b):
            d = piv[k][k]
            for q in range(k):
                d = d - low[k][q] * low[k][q]
            inv_diag[k] = lax.rsqrt(d)
            for l in range(k + 1, b):
                v = piv[l][k]
                for q in range(k):
                    v = v - low[l][q] * low[k][q]
                low[l][k] = v * inv_diag[k]

        def solve(rows):
            out = []
            for l in range(b):
                v = rows[l]
                for q in range(l):
                    v = v - low[l][q] * out[q]
                out.append(v * inv_diag[l])
            return out

        def solve_back(rows):
            out = [None] * b
            for l in reversed(range(b)):
                v = rows[l]
                for q in range(l + 1, b):
                    v = v - low[q][l] * out[q]
                out[l] = v * inv_diag[l]
            return out

        x = solve(rows_m)
        store_rows(j0, x)
        if j0 + b == TILE:
            break
        va, vm = solve_back(solve(rows_a)), solve_back(x)
        drop = (j0 + b) // sub * sub - done
        if drop:
            a, m, done = a[drop:], m[drop:], done + drop
        height = TILE - done
        da = dm = None
        for k in range(b):
            col = jnp.broadcast_to(a[:, j0 + k : j0 + k + 1], (height, TILE))
            if done < j0 + b:
                col = jnp.where(line[:height] >= j0 + b - done, col, 0.0)
            ta = col * jnp.broadcast_to(va[k][0:1], (height, TILE))
            tm = col * jnp.broadcast_to(vm[k][0:1], (height, TILE))
            da, dm = (ta, tm) if k == 0 else (da + ta, dm + tm)
        a, m = a - da, m - dm


def split(x):
    high = x.astype(jnp.bfloat16)
    return high, (x - high.astype(jnp.float32)).astype(jnp.bfloat16)


def mul(x, y, transposed=False):
    dims = (((1,), (1 if transposed else 0,)), ((), ()))
    return lax.dot_general(x, y, dims, preferred_element_type=jnp.float32)


def mul3(x, y, transposed=False):
    xh, xl = split(x)
    yh, yl = split(y)
    return mul(xh, yh, transposed) + (mul(xh, yl, transposed) + mul(xl, yh, transposed))


def factor_leading(lead, work, inverse, lower, block_inv, inv_high, inv_low, between):
    width = WIDTH
    work[...] = lead[...].astype(jnp.float32)
    row_of = lax.broadcasted_iota(jnp.int32, (width, width), 0)
    col_of = lax.broadcasted_iota(jnp.int32, (width, width), 1)
    inverse[...] = jnp.where(row_of == col_of, 1.0, 0.0).astype(jnp.float32)

    def store_rows(j0, x):
        for k in range(len(x)):
            block_inv[j0 + k : j0 + k + 1, :] = x[k][0:1, :]

    def step(kb, _):
        between(kb)
        o = pl.multiple_of(kb * TILE, TILE)
        here = pl.ds(o, TILE)
        invert_block(work[here, here], store_rows)
        d_inv = block_inv[...]
        below = mul3(work[:, here], d_inv, True)
        line = lax.broadcasted_iota(jnp.int32, (width, TILE), 0)
        lane = lax.broadcasted_iota(jnp.int32, (width, TILE), 1)
        lower[:, here] = jnp.where(line >= lane + o, below, 0.0)
        below = jnp.where(line >= o + TILE, below, 0.0)
        x_rows = mul3(d_inv, inverse[here, :])
        inverse[here, :] = x_rows
        work[...] = work[...] - mul3(below, below, True)
        inverse[...] = inverse[...] - mul3(below, x_rows)
        return 0

    lax.fori_loop(0, PANEL, step, 0)
    high, low = split(inverse[...])
    inv_high[...] = high
    inv_low[...] = low


def update_kernel(inv_high, inv_low, lower, top, panel, front, out, right):
    row_id = lax.axis_index("row")
    block_id = lax.axis_index("sub") * lax.axis_size("col") + lax.axis_index("col")
    tops = top[...]
    right[...] = mul(inv_high[...], tops) + mul(inv_low[...], tops)
    chunk = 128

    @pl.loop(0, panel.shape[0] // chunk)
    def _(t):
        rows = pl.ds(pl.multiple_of(t * chunk, chunk), chunk)
        a_rows = panel[rows, :]
        f_rows = mul(a_rows, inv_high[...], True) + mul(a_rows, inv_low[...], True)
        head = (row_id == 0) & (t < WIDTH // chunk)

        @pl.when(block_id == 0)
        def _():
            out[rows, :] = f_rows

            @pl.when(head)
            def _():
                out[rows, :] = lower[rows, :]

        @pl.when(block_id != 0)
        def _():
            @pl.when(head)
            def _():
                out[rows, :] = front[rows, :]

            @pl.when(jnp.logical_not(head))
            def _():
                out[rows, :] = front[rows, :] - mul3(f_rows, right[...])


def apply_update(inv_high, inv_low, lower, top, panel, front):
    vmem = pl.BlockSpec(memory_space=pltpu.VMEM)
    return pl.pallas_call(
        update_kernel,
        out_shape=jax.ShapeDtypeStruct(front.shape, jnp.float32),
        in_specs=[vmem] * 6,
        out_specs=vmem,
        scratch_shapes=[pltpu.VMEM((WIDTH, WIDTH), jnp.float32)],
        name="apply_update",
    )(inv_high, inv_low, lower, top, panel, front)


def body(child_update, parent_front, tile_map):
    tile_len = TILE
    panel_tiles = PANEL
    sub_count = lax.axis_size("sub")
    row_count = lax.axis_size("row")
    col_count = lax.axis_size("col")
    sub_id = lax.axis_index("sub")
    row_id = lax.axis_index("row")
    col_id = lax.axis_index("col")
    child_rows = child_update.shape[0] // tile_len
    child_cols = child_update.shape[1] // tile_len
    front_rows = parent_front.shape[0] // tile_len
    own_map = lax.dynamic_index_in_dim(tile_map, sub_id, 0, keepdims=False)
    own_cols = lax.dynamic_index_in_dim(
        own_map.reshape(child_cols, col_count), col_id, 1, keepdims=False
    )
    live_cols = own_cols >= 0
    destination = jnp.floor_divide(jnp.floor_divide(own_cols, panel_tiles), col_count)
    slot_index = jnp.remainder(own_cols, panel_tiles)
    dest_hit = destination[None, :] == jnp.arange(sub_count, dtype=jnp.int32)[:, None]
    slot_hit = slot_index[None, :] == jnp.arange(panel_tiles, dtype=jnp.int32)[:, None]
    select = (live_cols[None, None, :] & dest_hit[:, None, :] & slot_hit[None, :, :]).astype(
        jnp.bfloat16
    )
    column_slabs = child_update.reshape(child_rows * tile_len, child_cols, tile_len)
    payload = jnp.einsum(
        "dqk,rky->dqry", select, column_slabs, preferred_element_type=jnp.float32
    ).astype(jnp.bfloat16)
    maps_rows = lax.dynamic_index_in_dim(
        tile_map.reshape(sub_count, child_rows, row_count), row_id, 2, keepdims=False
    )
    local_row = jnp.floor_divide(
        jnp.floor_divide(maps_rows, panel_tiles), row_count
    ) * panel_tiles + jnp.remainder(maps_rows, panel_tiles)
    row_hit = (maps_rows[:, :, None] >= 0) & (
        local_row[:, :, None] == jnp.arange(front_rows, dtype=jnp.int32)[None, None, :]
    )
    place_row = row_hit.astype(jnp.bfloat16)
    own_place = lax.dynamic_index_in_dim(place_row, sub_id, 0, keepdims=False)[:, :panel_tiles]
    own_grid = payload[0].reshape(panel_tiles, child_rows, tile_len, tile_len)
    contribution = (
        jnp.einsum("ka,qkyx->ayqx", own_place, own_grid, preferred_element_type=jnp.float32)
        .astype(jnp.bfloat16)
        .reshape(WIDTH, WIDTH)
    )
    lead = spread_leading(
        contribution, parent_front[:WIDTH], sub_count, row_count, col_count
    )
    arrived = lax.all_to_all(payload, "sub", split_axis=0, concat_axis=0, tiled=True)
    slot_count = arrived.shape[1]
    grid = arrived.reshape(sub_count, slot_count, child_rows, tile_len, tile_len)
    spread = jnp.einsum("ska,sqkyx->ayqx", place_row, grid, preferred_element_type=jnp.float32)
    placed = spread.reshape(front_rows * tile_len, slot_count * tile_len)
    front_local = parent_front.astype(jnp.float32) + placed
    panel, top, inv_high, inv_low, lower = spread_panels(
        front_local.astype(jnp.bfloat16), lead, sub_count, row_count, col_count
    )
    return apply_update(inv_high, inv_low, lower, top, panel, front_local)


def solution(mesh):
    in_specs = (P(("sub", "row"), "col"), P("row", ("sub", "col")), P())
    out_specs = P("row", ("sub", "col"))
    return jax.shard_map(body, mesh=mesh, in_specs=in_specs, out_specs=out_specs, check_vma=False)
```

```python
import functools

import jax
import jax.numpy as jnp
from jax import lax
from jax.experimental import pallas as pl
from jax.experimental.pallas import tpu as pltpu
from jax.sharding import PartitionSpec as P

TILE = 128
PANEL = 4
WIDTH = TILE * PANEL
MESH = pl.DeviceIdType.MESH
GROUP = 8
PIECE = WIDTH // GROUP


def remote(src, dst, send_sem, recv_sem, device):
    return pltpu.make_async_remote_copy(
        src_ref=src,
        dst_ref=dst,
        send_sem=send_sem,
        recv_sem=recv_sem,
        device_id=device,
        device_id_type=MESH,
    )


def each(count, skip, fn):
    def step(i, _):
        @pl.when(i != skip)
        def _():
            fn(i)

        return 0

    lax.fori_loop(0, count, step, 0)


def farthest_first(count):
    return sorted(range(1, count), key=lambda k: -min(k, count - k))


def spread_kernel(
    n_sub,
    n_row,
    n_col,
    front,
    panel,
    top,
    inv_high,
    inv_low,
    lower,
    lead,
    work,
    inverse,
    block_inv,
    local_sem,
    top_send,
    top_cross,
    top_gather,
    top_recv,
    panel_col,
    panel_sub,
    panel_recv,
    panel_far,
    ring_right,
    ring_left,
    lead_sub,
    lead_col,
    lead_gather,
    lead_recv,
):
    s, r, c = lax.axis_index("sub"), lax.axis_index("row"), lax.axis_index("col")
    p = s * n_col + c
    half, i = r // GROUP, r % GROUP
    depth = front.shape[0] // n_col

    def at_group(j):
        return (s, half * GROUP + j, c)

    def top_piece(j):
        return top.at[pl.ds(pl.multiple_of(j * PIECE, PIECE), PIECE)]

    def lead_piece(j):
        return lead.at[pl.ds(pl.multiple_of(j * PIECE, PIECE), PIECE)]

    def panel_piece(q):
        return panel.at[pl.ds(pl.multiple_of(q * depth, depth), depth)]

    def front_piece(q):
        return front.at[pl.ds(pl.multiple_of(q * depth, depth), depth)]

    def front_top(j):
        return front.at[pl.ds(pl.multiple_of(j * PIECE, PIECE), PIECE)]

    barrier = pltpu.get_barrier_semaphore()
    across = (s, (1 - half) * GROUP + i, c)

    def greet(device):
        pl.semaphore_signal(barrier, inc=1, device_id=device, device_id_type=MESH)

    each(n_sub, s, lambda k: greet((k, r, c)))
    each(n_col, c, lambda k: greet((s, r, k)))
    each(GROUP, i, lambda j: greet(at_group(j)))
    greet(across)
    pl.semaphore_wait(barrier, n_sub - 1 + n_col - 1 + GROUP - 1 + 1)

    top_scatter = lambda j: remote(
        front_top(j), top_piece(j), top_send.at[j], top_recv.at[j], at_group(j)
    )
    panel_along = lambda k: remote(
        front_piece(k), panel_piece(k), panel_col.at[k], panel_recv.at[k], (0, r, k)
    )
    root_down = lambda k: remote(
        front_piece(0), panel_piece(0), panel_sub.at[k], panel_recv.at[0], (k, r, 0)
    )
    panel_down = lambda k: remote(
        panel_piece(c), panel_piece(c), panel_sub.at[k], panel_recv.at[c], (k, r, c)
    )
    right, left = (c + 1) % n_col, (c + n_col - 1) % n_col
    last = n_col // 2

    def from_left(t):
        return (c + n_col - t) % n_col

    def from_right(t):
        return (c + t) % n_col

    def ring_copies(t):
        go_right, go_left = panel_piece(from_left(t - 1)), panel_piece(from_right(t - 1))
        left_sem = panel_recv.at[from_right(t - 1)]
        if t == last:
            go_right = go_right.at[pl.ds(0, depth // 2)]
            go_left = go_left.at[pl.ds(depth // 2, depth // 2)]
            left_sem = panel_far
        return (
            remote(
                go_right, go_right, ring_right.at[t], panel_recv.at[from_left(t - 1)], (s, r, right)
            ),
            remote(go_left, go_left, ring_left.at[t], left_sem, (s, r, left)),
        )

    to_right, to_left = (s != 0) | (right != 0), (s != 0) | (left != 0)

    def ring_step(t):
        @pl.when((p != 0) & ((t > 1) | (s != 0)))
        def _():
            arrived(panel_piece(from_left(t - 1)), panel_recv.at[from_left(t - 1)])
            if t > 1:
                arrived(panel_piece(from_right(t - 1)), panel_recv.at[from_right(t - 1)])

        go_right, go_left = ring_copies(t)
        pl.when(to_right)(go_right.start)
        pl.when(to_left)(go_left.start)

    top_over = remote(top_piece(i), top_piece(i), top_cross, top_recv.at[i], across)
    top_share = lambda j: remote(
        top_piece(i), top_piece(i), top_gather.at[j], top_recv.at[i], at_group(j)
    )
    lead_down = lambda k: remote(
        top_piece(i), lead_piece(i), lead_sub.at[k], lead_recv.at[i], (k, r, 0)
    )
    lead_along = lambda k: remote(
        top_piece(i), lead_piece(i), lead_col.at[k], lead_recv.at[i], (s, r, k)
    )
    lead_forward = lambda k: remote(
        lead_piece(i), lead_piece(i), lead_col.at[k], lead_recv.at[i], (s, r, k)
    )
    lead_share = lambda j: remote(
        lead_piece(i), lead_piece(i), lead_gather.at[j], lead_recv.at[i], at_group(j)
    )
    own_top = pltpu.make_async_copy(front.at[pl.ds(0, WIDTH)], top, local_sem.at[0])
    own_panel = pltpu.make_async_copy(front, panel, local_sem.at[1])
    own_lead = pltpu.make_async_copy(top, lead, local_sem.at[2])

    def arrived(piece, sem):
        pltpu.make_async_copy(piece, piece, sem).wait()

    def share_top():
        each(GROUP, i, lambda j: pl.when((j != 0) | (half != 0))(lambda: top_share(j).start()))

    @pl.when(r == 0)
    def _():
        own_top.start()
        each(GROUP, 0, lambda j: top_scatter(j).start())
        own_top.wait()

    @pl.when((r != 0) & (half == 0))
    def _():
        arrived(top_piece(i), top_recv.at[i])

    @pl.when(half == 0)
    def _():
        top_over.start()

    @pl.when(p == 0)
    def _():
        @pl.when(half != 0)
        def _():
            arrived(top_piece(i), top_recv.at[i])

        each(n_sub, 0, lambda k: lead_down(k).start())
        for k in farthest_first(n_col):
            lead_along(k).start()
        own_panel.start()
        each(n_sub, 0, lambda k: root_down(k).start())
        for k in farthest_first(n_col):
            panel_along(k).start()
        share_top()
        own_panel.wait()

    @pl.when(p != 0)
    def _():
        arrived(lead_piece(i), lead_recv.at[i])

        @pl.when(c == 0)
        def _():
            for k in farthest_first(n_col):
                lead_forward(k).start()

        for k in farthest_first(GROUP):
            lead_share((i + k) % GROUP).start()

        @pl.when(s == 0)
        def _():
            arrived(panel_piece(c), panel_recv.at[c])
            each(n_sub, 0, lambda k: panel_down(k).start())

    def all_of_top():
        each(GROUP, i, lambda j: arrived(top_piece(j), top_recv.at[j]))

    pl.when((r != 0) & (p == 0))(all_of_top)

    @pl.when(p == 0)
    def _():
        own_lead.start()
        own_lead.wait()

    @pl.when(p != 0)
    def _():
        each(GROUP, i, lambda j: arrived(lead_piece(j), lead_recv.at[j]))

    def pass_top():
        @pl.when(p != 0)
        def _():
            @pl.when(half != 0)
            def _():
                arrived(top_piece(i), top_recv.at[i])

            share_top()

    def between(kb, late):
        if late:
            for t in range(1, last):
                pl.when(kb == t)(functools.partial(ring_step, t + 1))
        else:
            pl.when(kb == 0)(pass_top)
            pl.when(kb == 1)(functools.partial(ring_step, 1))

    factor_leading(lead, work, inverse, lower, block_inv, inv_high, inv_low, between)

    pl.when((r != 0) & (p != 0))(all_of_top)

    @pl.when(p != 0)
    def _():
        low = panel_piece(from_left(last)).at[pl.ds(0, depth // 2)]
        high = panel_piece(from_left(last)).at[pl.ds(depth // 2, depth // 2)]
        arrived(low, panel_recv.at[from_left(last)])
        arrived(high, panel_far)

    @pl.when(r == 0)
    def _():
        each(GROUP, 0, lambda j: top_scatter(j).wait_send())

    @pl.when(half == 0)
    def _():
        top_over.wait_send()
        each(GROUP, i, lambda j: pl.when(j != 0)(lambda: top_share(j).wait_send()))

    @pl.when(half != 0)
    def _():
        each(GROUP, i, lambda j: top_share(j).wait_send())

    @pl.when(p == 0)
    def _():
        each(n_sub, 0, lambda k: root_down(k).wait_send())
        each(n_col, 0, lambda k: panel_along(k).wait_send())
        each(n_sub, 0, lambda k: lead_down(k).wait_send())
        each(n_col, 0, lambda k: lead_along(k).wait_send())

    @pl.when(p != 0)
    def _():
        @pl.when(s == 0)
        def _():
            each(n_sub, 0, lambda k: panel_down(k).wait_send())

        @pl.when(c == 0)
        def _():
            each(n_col, 0, lambda k: lead_forward(k).wait_send())

        each(GROUP, i, lambda j: lead_share(j).wait_send())

    for t in range(1, last + 1):
        go_right, go_left = ring_copies(t)
        pl.when(to_right)(go_right.wait_send)
        pl.when(to_left)(go_left.wait_send)


def spread_panels(front16, n_sub, n_row, n_col):
    rows, width = front16.shape
    vmem = pl.BlockSpec(memory_space=pltpu.VMEM)
    dma = pltpu.SemaphoreType.DMA
    return pl.pallas_call(
        functools.partial(spread_kernel, n_sub, n_row, n_col),
        out_shape=(
            jax.ShapeDtypeStruct((rows, width), jnp.bfloat16),
            jax.ShapeDtypeStruct((WIDTH, width), jnp.bfloat16),
            jax.ShapeDtypeStruct((WIDTH, WIDTH), jnp.bfloat16),
            jax.ShapeDtypeStruct((WIDTH, WIDTH), jnp.bfloat16),
            jax.ShapeDtypeStruct((WIDTH, WIDTH), jnp.float32),
        ),
        in_specs=[vmem],
        out_specs=(vmem,) * 5,
        scratch_shapes=[
            pltpu.VMEM((WIDTH, WIDTH), jnp.bfloat16),
            pltpu.VMEM((WIDTH, WIDTH), jnp.float32),
            pltpu.VMEM((WIDTH, WIDTH), jnp.float32),
            pltpu.VMEM((TILE, TILE), jnp.float32),
            dma((3,)),
            dma((GROUP,)),
            dma(()),
            dma((GROUP,)),
            dma((GROUP,)),
            dma((n_col,)),
            dma((n_sub,)),
            dma((n_col,)),
            dma(()),
            dma((n_col,)),
            dma((n_col,)),
            dma((n_sub,)),
            dma((n_col,)),
            dma((GROUP,)),
            dma((GROUP,)),
        ],
        compiler_params=pltpu.CompilerParams(collective_id=0, has_side_effects=True),
        name="spread_panels",
    )(front16)


def invert_block(block, store_rows):
    sub = 8
    b = 4
    line = lax.broadcasted_iota(jnp.int32, (TILE, TILE), 0)
    lane = lax.broadcasted_iota(jnp.int32, (TILE, TILE), 1)
    a = block
    m = jnp.where(lane == line, 1.0, 0.0).astype(jnp.float32)
    done = 0
    for j0 in range(0, TILE, b):
        i0 = j0 - done
        rows_a = [jnp.broadcast_to(a[i0 + k : i0 + k + 1, :], (sub, TILE)) for k in range(b)]
        rows_m = [jnp.broadcast_to(m[i0 + k : i0 + k + 1, :], (sub, TILE)) for k in range(b)]
        piv = [
            [
                jnp.broadcast_to(rows_a[l][:, j0 + k : j0 + k + 1], (sub, TILE))
                for k in range(l + 1)
            ]
            for l in range(b)
        ]
        low = [[None] * b for _ in range(b)]
        inv_diag = [None] * b
        for k in range(b):
            d = piv[k][k]
            for q in range(k):
                d = d - low[k][q] * low[k][q]
            inv_diag[k] = lax.rsqrt(d)
            for l in range(k + 1, b):
                v = piv[l][k]
                for q in range(k):
                    v = v - low[l][q] * low[k][q]
                low[l][k] = v * inv_diag[k]

        def solve(rows):
            out = []
            for l in range(b):
                v = rows[l]
                for q in range(l):
                    v = v - low[l][q] * out[q]
                out.append(v * inv_diag[l])
            return out

        def solve_back(rows):
            out = [None] * b
            for l in reversed(range(b)):
                v = rows[l]
                for q in range(l + 1, b):
                    v = v - low[q][l] * out[q]
                out[l] = v * inv_diag[l]
            return out

        x = solve(rows_m)
        store_rows(j0, x)
        if j0 + b == TILE:
            break
        va, vm = solve_back(solve(rows_a)), solve_back(x)
        drop = (j0 + b) // sub * sub - done
        if drop:
            a, m, done = a[drop:], m[drop:], done + drop
        height = TILE - done
        da = dm = None
        for k in range(b):
            col = jnp.broadcast_to(a[:, j0 + k : j0 + k + 1], (height, TILE))
            if done < j0 + b:
                col = jnp.where(line[:height] >= j0 + b - done, col, 0.0)
            ta = col * jnp.broadcast_to(va[k][0:1], (height, TILE))
            tm = col * jnp.broadcast_to(vm[k][0:1], (height, TILE))
            da, dm = (ta, tm) if k == 0 else (da + ta, dm + tm)
        a, m = a - da, m - dm


def split(x):
    high = x.astype(jnp.bfloat16)
    return high, (x - high.astype(jnp.float32)).astype(jnp.bfloat16)


def mul(x, y, transposed=False):
    dims = (((1,), (1 if transposed else 0,)), ((), ()))
    return lax.dot_general(x, y, dims, preferred_element_type=jnp.float32)


def mul3(x, y, transposed=False):
    xh, xl = split(x)
    yh, yl = split(y)
    return mul(xh, yh, transposed) + (mul(xh, yl, transposed) + mul(xl, yh, transposed))


def factor_leading(lead, work, inverse, lower, block_inv, inv_high, inv_low, between):
    width = WIDTH
    work[...] = lead[...].astype(jnp.float32)
    row_of = lax.broadcasted_iota(jnp.int32, (width, width), 0)
    col_of = lax.broadcasted_iota(jnp.int32, (width, width), 1)
    inverse[...] = jnp.where(row_of == col_of, 1.0, 0.0).astype(jnp.float32)

    def store_rows(j0, x):
        for k in range(len(x)):
            block_inv[j0 + k : j0 + k + 1, :] = x[k][0:1, :]

    def step(kb, _):
        between(kb, False)
        o = pl.multiple_of(kb * TILE, TILE)
        here = pl.ds(o, TILE)
        invert_block(work[here, here], store_rows)
        between(kb, True)
        d_inv = block_inv[...]
        below = mul3(work[:, here], d_inv, True)
        line = lax.broadcasted_iota(jnp.int32, (width, TILE), 0)
        lane = lax.broadcasted_iota(jnp.int32, (width, TILE), 1)
        lower[:, here] = jnp.where(line >= lane + o, below, 0.0)
        below = jnp.where(line >= o + TILE, below, 0.0)
        x_rows = mul3(d_inv, inverse[here, :])
        inverse[here, :] = x_rows
        work[...] = work[...] - mul3(below, below, True)
        inverse[...] = inverse[...] - mul3(below, x_rows)
        return 0

    lax.fori_loop(0, PANEL, step, 0)
    high, low = split(inverse[...])
    inv_high[...] = high
    inv_low[...] = low


def update_kernel(inv_high, inv_low, lower, top, panel, front, out, right):
    row_id = lax.axis_index("row")
    block_id = lax.axis_index("sub") * lax.axis_size("col") + lax.axis_index("col")
    tops = top[...]
    right[...] = mul(inv_high[...], tops) + mul(inv_low[...], tops)
    chunk = 128

    @pl.loop(0, panel.shape[0] // chunk)
    def _(t):
        rows = pl.ds(pl.multiple_of(t * chunk, chunk), chunk)
        a_rows = panel[rows, :]
        f_rows = mul(a_rows, inv_high[...], True) + mul(a_rows, inv_low[...], True)
        head = (row_id == 0) & (t < WIDTH // chunk)

        @pl.when(block_id == 0)
        def _():
            out[rows, :] = f_rows

            @pl.when(head)
            def _():
                out[rows, :] = lower[rows, :]

        @pl.when(block_id != 0)
        def _():
            @pl.when(head)
            def _():
                out[rows, :] = front[rows, :]

            @pl.when(jnp.logical_not(head))
            def _():
                out[rows, :] = front[rows, :] - mul3(f_rows, right[...])


def apply_update(inv_high, inv_low, lower, top, panel, front):
    vmem = pl.BlockSpec(memory_space=pltpu.VMEM)
    return pl.pallas_call(
        update_kernel,
        out_shape=jax.ShapeDtypeStruct(front.shape, jnp.float32),
        in_specs=[vmem] * 6,
        out_specs=vmem,
        scratch_shapes=[pltpu.VMEM((WIDTH, WIDTH), jnp.float32)],
        name="apply_update",
    )(inv_high, inv_low, lower, top, panel, front)


def body(child_update, parent_front, tile_map):
    tile_len = TILE
    panel_tiles = PANEL
    sub_count = lax.axis_size("sub")
    row_count = lax.axis_size("row")
    col_count = lax.axis_size("col")
    sub_id = lax.axis_index("sub")
    row_id = lax.axis_index("row")
    col_id = lax.axis_index("col")
    child_rows = child_update.shape[0] // tile_len
    child_cols = child_update.shape[1] // tile_len
    front_rows = parent_front.shape[0] // tile_len
    own_map = lax.dynamic_index_in_dim(tile_map, sub_id, 0, keepdims=False)
    own_cols = lax.dynamic_index_in_dim(
        own_map.reshape(child_cols, col_count), col_id, 1, keepdims=False
    )
    live_cols = own_cols >= 0
    destination = jnp.floor_divide(jnp.floor_divide(own_cols, panel_tiles), col_count)
    slot_index = jnp.remainder(own_cols, panel_tiles)
    dest_hit = destination[None, :] == jnp.arange(sub_count, dtype=jnp.int32)[:, None]
    slot_hit = slot_index[None, :] == jnp.arange(panel_tiles, dtype=jnp.int32)[:, None]
    select = (live_cols[None, None, :] & dest_hit[:, None, :] & slot_hit[None, :, :]).astype(
        jnp.bfloat16
    )
    column_slabs = child_update.reshape(child_rows * tile_len, child_cols, tile_len)
    payload = jnp.einsum(
        "dqk,rky->dqry", select, column_slabs, preferred_element_type=jnp.float32
    ).astype(jnp.bfloat16)
    maps_rows = lax.dynamic_index_in_dim(
        tile_map.reshape(sub_count, child_rows, row_count), row_id, 2, keepdims=False
    )
    local_row = jnp.floor_divide(
        jnp.floor_divide(maps_rows, panel_tiles), row_count
    ) * panel_tiles + jnp.remainder(maps_rows, panel_tiles)
    row_hit = (maps_rows[:, :, None] >= 0) & (
        local_row[:, :, None] == jnp.arange(front_rows, dtype=jnp.int32)[None, None, :]
    )
    place_row = row_hit.astype(jnp.bfloat16)
    arrived = lax.all_to_all(payload, "sub", split_axis=0, concat_axis=0, tiled=True)
    slot_count = arrived.shape[1]
    grid = arrived.reshape(sub_count, slot_count, child_rows, tile_len, tile_len)
    spread = jnp.einsum("ska,sqkyx->ayqx", place_row, grid, preferred_element_type=jnp.float32)
    placed = spread.reshape(front_rows * tile_len, slot_count * tile_len)
    front_local = parent_front.astype(jnp.float32) + placed
    panel, top, inv_high, inv_low, lower = spread_panels(
        front_local.astype(jnp.bfloat16), sub_count, row_count, col_count
    )
    return apply_update(inv_high, inv_low, lower, top, panel, front_local)


def solution(mesh):
    in_specs = (P(("sub", "row"), "col"), P("row", ("sub", "col")), P())
    out_specs = P("row", ("sub", "col"))
    return jax.shard_map(body, mesh=mesh, in_specs=in_specs, out_specs=out_specs, check_vma=False)
```

```python
import functools

import jax
import jax.numpy as jnp
from jax import lax
from jax.experimental import pallas as pl
from jax.experimental.pallas import tpu as pltpu
from jax.sharding import PartitionSpec as P

TILE = 128
PANEL = 4
WIDTH = TILE * PANEL
MESH = pl.DeviceIdType.MESH
GROUP = 8
PIECE = WIDTH // GROUP


def remote(src, dst, send_sem, recv_sem, device):
    return pltpu.make_async_remote_copy(
        src_ref=src,
        dst_ref=dst,
        send_sem=send_sem,
        recv_sem=recv_sem,
        device_id=device,
        device_id_type=MESH,
    )


def each(count, skip, fn):
    def step(i, _):
        @pl.when(i != skip)
        def _():
            fn(i)

        return 0

    lax.fori_loop(0, count, step, 0)


def farthest_first(count):
    return sorted(range(1, count), key=lambda k: -min(k, count - k))


def spread_kernel(
    n_sub,
    n_row,
    n_col,
    front,
    panel,
    top,
    inv_high,
    inv_low,
    lower,
    lead,
    work,
    inverse,
    block_inv,
    local_sem,
    top_send,
    top_cross,
    top_gather,
    top_recv,
    panel_col,
    panel_sub,
    panel_recv,
    panel_far,
    ring_right,
    ring_left,
    lead_sub,
    lead_col,
    lead_gather,
    lead_recv,
):
    s, r, c = lax.axis_index("sub"), lax.axis_index("row"), lax.axis_index("col")
    p = s * n_col + c
    half, i = r // GROUP, r % GROUP
    depth = front.shape[0] // n_col

    def at_group(j):
        return (s, half * GROUP + j, c)

    def top_piece(j):
        return top.at[pl.ds(pl.multiple_of(j * PIECE, PIECE), PIECE)]

    def lead_piece(j):
        return lead.at[pl.ds(pl.multiple_of(j * PIECE, PIECE), PIECE)]

    def panel_piece(q):
        return panel.at[pl.ds(pl.multiple_of(q * depth, depth), depth)]

    def front_piece(q):
        return front.at[pl.ds(pl.multiple_of(q * depth, depth), depth)]

    def front_top(j):
        return front.at[pl.ds(pl.multiple_of(j * PIECE, PIECE), PIECE)]

    barrier = pltpu.get_barrier_semaphore()
    across = (s, (1 - half) * GROUP + i, c)

    def greet(device):
        pl.semaphore_signal(barrier, inc=1, device_id=device, device_id_type=MESH)

    each(n_sub, s, lambda k: greet((k, r, c)))
    each(n_col, c, lambda k: greet((s, r, k)))
    each(GROUP, i, lambda j: greet(at_group(j)))
    greet(across)
    pl.semaphore_wait(barrier, n_sub - 1 + n_col - 1 + GROUP - 1 + 1)

    top_scatter = lambda j: remote(
        front_top(j), top_piece(j), top_send.at[j], top_recv.at[j], at_group(j)
    )
    panel_along = lambda k: remote(
        front_piece(k), panel_piece(k), panel_col.at[k], panel_recv.at[k], (0, r, k)
    )
    root_down = lambda k: remote(
        front_piece(0), panel_piece(0), panel_sub.at[k], panel_recv.at[0], (k, r, 0)
    )
    panel_down = lambda k: remote(
        panel_piece(c), panel_piece(c), panel_sub.at[k], panel_recv.at[c], (k, r, c)
    )
    right, left = (c + 1) % n_col, (c + n_col - 1) % n_col
    last = n_col // 2

    def from_left(t):
        return (c + n_col - t) % n_col

    def from_right(t):
        return (c + t) % n_col

    def ring_copies(t):
        go_right, go_left = panel_piece(from_left(t - 1)), panel_piece(from_right(t - 1))
        left_sem = panel_recv.at[from_right(t - 1)]
        if t == last:
            go_right = go_right.at[pl.ds(0, depth // 2)]
            go_left = go_left.at[pl.ds(depth // 2, depth // 2)]
            left_sem = panel_far
        return (
            remote(
                go_right, go_right, ring_right.at[t], panel_recv.at[from_left(t - 1)], (s, r, right)
            ),
            remote(go_left, go_left, ring_left.at[t], left_sem, (s, r, left)),
        )

    to_right, to_left = (s != 0) | (right != 0), (s != 0) | (left != 0)

    def ring_step(t):
        @pl.when((p != 0) & ((t > 1) | (s != 0)))
        def _():
            arrived(panel_piece(from_left(t - 1)), panel_recv.at[from_left(t - 1)])
            if t > 1:
                arrived(panel_piece(from_right(t - 1)), panel_recv.at[from_right(t - 1)])

        go_right, go_left = ring_copies(t)
        pl.when(to_right)(go_right.start)
        pl.when(to_left)(go_left.start)

    top_over = remote(top_piece(i), top_piece(i), top_cross, top_recv.at[i], across)
    top_share = lambda j: remote(
        top_piece(i), top_piece(i), top_gather.at[j], top_recv.at[i], at_group(j)
    )
    lead_down = lambda k: remote(
        top_piece(i), lead_piece(i), lead_sub.at[k], lead_recv.at[i], (k, r, 0)
    )
    lead_along = lambda k: remote(
        top_piece(i), lead_piece(i), lead_col.at[k], lead_recv.at[i], (s, r, k)
    )
    lead_forward = lambda k: remote(
        lead_piece(i), lead_piece(i), lead_col.at[k], lead_recv.at[i], (s, r, k)
    )
    lead_share = lambda j: remote(
        lead_piece(i), lead_piece(i), lead_gather.at[j], lead_recv.at[i], at_group(j)
    )
    own_top = pltpu.make_async_copy(front.at[pl.ds(0, WIDTH)], top, local_sem.at[0])
    own_panel = pltpu.make_async_copy(front, panel, local_sem.at[1])
    own_lead = pltpu.make_async_copy(top, lead, local_sem.at[2])

    def arrived(piece, sem):
        pltpu.make_async_copy(piece, piece, sem).wait()

    def share_top():
        each(GROUP, i, lambda j: pl.when((j != 0) | (half != 0))(lambda: top_share(j).start()))

    @pl.when(r == 0)
    def _():
        own_top.start()
        each(GROUP, 0, lambda j: top_scatter(j).start())
        own_top.wait()

    @pl.when((r != 0) & (half == 0))
    def _():
        arrived(top_piece(i), top_recv.at[i])

    @pl.when(half == 0)
    def _():
        top_over.start()

    @pl.when(p == 0)
    def _():
        @pl.when(half != 0)
        def _():
            arrived(top_piece(i), top_recv.at[i])

        each(n_sub, 0, lambda k: lead_down(k).start())
        for k in farthest_first(n_col):
            lead_along(k).start()
        own_panel.start()
        each(n_sub, 0, lambda k: root_down(k).start())
        for k in farthest_first(n_col):
            panel_along(k).start()
        share_top()
        own_panel.wait()

    @pl.when(p != 0)
    def _():
        arrived(lead_piece(i), lead_recv.at[i])

        @pl.when(c == 0)
        def _():
            for k in farthest_first(n_col):
                lead_forward(k).start()

        for k in farthest_first(GROUP):
            lead_share((i + k) % GROUP).start()

        @pl.when(s == 0)
        def _():
            arrived(panel_piece(c), panel_recv.at[c])
            each(n_sub, 0, lambda k: panel_down(k).start())

    def all_of_top():
        each(GROUP, i, lambda j: arrived(top_piece(j), top_recv.at[j]))

    pl.when((r != 0) & (p == 0))(all_of_top)

    @pl.when(p == 0)
    def _():
        own_lead.start()
        own_lead.wait()

    @pl.when(p != 0)
    def _():
        each(GROUP, i, lambda j: arrived(lead_piece(j), lead_recv.at[j]))

    def pass_top():
        @pl.when(p != 0)
        def _():
            @pl.when(half != 0)
            def _():
                arrived(top_piece(i), top_recv.at[i])

            share_top()

    def between(kb, late):
        if late:
            for t in range(1, last):
                pl.when(kb == t)(functools.partial(ring_step, t + 1))
        else:
            pl.when(kb == 0)(pass_top)
            pl.when(kb == 1)(functools.partial(ring_step, 1))

    factor_leading(lead, work, inverse, lower, block_inv, inv_high, inv_low, between)

    pl.when((r != 0) & (p != 0))(all_of_top)

    @pl.when(p != 0)
    def _():
        low = panel_piece(from_left(last)).at[pl.ds(0, depth // 2)]
        high = panel_piece(from_left(last)).at[pl.ds(depth // 2, depth // 2)]
        arrived(low, panel_recv.at[from_left(last)])
        arrived(high, panel_far)

    @pl.when(r == 0)
    def _():
        each(GROUP, 0, lambda j: top_scatter(j).wait_send())

    @pl.when(half == 0)
    def _():
        top_over.wait_send()
        each(GROUP, i, lambda j: pl.when(j != 0)(lambda: top_share(j).wait_send()))

    @pl.when(half != 0)
    def _():
        each(GROUP, i, lambda j: top_share(j).wait_send())

    @pl.when(p == 0)
    def _():
        each(n_sub, 0, lambda k: root_down(k).wait_send())
        each(n_col, 0, lambda k: panel_along(k).wait_send())
        each(n_sub, 0, lambda k: lead_down(k).wait_send())
        each(n_col, 0, lambda k: lead_along(k).wait_send())

    @pl.when(p != 0)
    def _():
        @pl.when(s == 0)
        def _():
            each(n_sub, 0, lambda k: panel_down(k).wait_send())

        @pl.when(c == 0)
        def _():
            each(n_col, 0, lambda k: lead_forward(k).wait_send())

        each(GROUP, i, lambda j: lead_share(j).wait_send())

    for t in range(1, last + 1):
        go_right, go_left = ring_copies(t)
        pl.when(to_right)(go_right.wait_send)
        pl.when(to_left)(go_left.wait_send)


def spread_panels(front16, n_sub, n_row, n_col):
    rows, width = front16.shape
    vmem = pl.BlockSpec(memory_space=pltpu.VMEM)
    dma = pltpu.SemaphoreType.DMA
    return pl.pallas_call(
        functools.partial(spread_kernel, n_sub, n_row, n_col),
        out_shape=(
            jax.ShapeDtypeStruct((rows, width), jnp.bfloat16),
            jax.ShapeDtypeStruct((WIDTH, width), jnp.bfloat16),
            jax.ShapeDtypeStruct((WIDTH, WIDTH), jnp.bfloat16),
            jax.ShapeDtypeStruct((WIDTH, WIDTH), jnp.bfloat16),
            jax.ShapeDtypeStruct((WIDTH, WIDTH), jnp.float32),
        ),
        in_specs=[vmem],
        out_specs=(vmem,) * 5,
        scratch_shapes=[
            pltpu.VMEM((WIDTH, WIDTH), jnp.bfloat16),
            pltpu.VMEM((WIDTH, WIDTH), jnp.float32),
            pltpu.VMEM((WIDTH, WIDTH), jnp.float32),
            pltpu.VMEM((TILE, TILE), jnp.float32),
            dma((3,)),
            dma((GROUP,)),
            dma(()),
            dma((GROUP,)),
            dma((GROUP,)),
            dma((n_col,)),
            dma((n_sub,)),
            dma((n_col,)),
            dma(()),
            dma((n_col,)),
            dma((n_col,)),
            dma((n_sub,)),
            dma((n_col,)),
            dma((GROUP,)),
            dma((GROUP,)),
        ],
        compiler_params=pltpu.CompilerParams(collective_id=0, has_side_effects=True),
        name="spread_panels",
    )(front16)


def invert_block(block, store_rows):
    sub = 8
    b = 4
    line = lax.broadcasted_iota(jnp.int32, (TILE, TILE), 0)
    lane = lax.broadcasted_iota(jnp.int32, (TILE, TILE), 1)
    a = block
    m = jnp.where(lane == line, 1.0, 0.0).astype(jnp.float32)
    done = 0
    for j0 in range(0, TILE, b):
        i0 = j0 - done
        rows_a = [jnp.broadcast_to(a[i0 + k : i0 + k + 1, :], (sub, TILE)) for k in range(b)]
        rows_m = [jnp.broadcast_to(m[i0 + k : i0 + k + 1, :], (sub, TILE)) for k in range(b)]
        piv = [
            [
                jnp.broadcast_to(rows_a[l][:, j0 + k : j0 + k + 1], (sub, TILE))
                for k in range(l + 1)
            ]
            for l in range(b)
        ]
        low = [[None] * b for _ in range(b)]
        inv_diag = [None] * b
        for k in range(b):
            d = piv[k][k]
            for q in range(k):
                d = d - low[k][q] * low[k][q]
            inv_diag[k] = lax.rsqrt(d)
            for l in range(k + 1, b):
                v = piv[l][k]
                for q in range(k):
                    v = v - low[l][q] * low[k][q]
                low[l][k] = v * inv_diag[k]

        def solve(rows):
            out = []
            for l in range(b):
                v = rows[l]
                for q in range(l):
                    v = v - low[l][q] * out[q]
                out.append(v * inv_diag[l])
            return out

        def solve_back(rows):
            out = [None] * b
            for l in reversed(range(b)):
                v = rows[l]
                for q in range(l + 1, b):
                    v = v - low[q][l] * out[q]
                out[l] = v * inv_diag[l]
            return out

        x = solve(rows_m)
        store_rows(j0, x)
        if j0 + b == TILE:
            break
        va, vm = solve_back(solve(rows_a)), solve_back(x)
        drop = (j0 + b) // sub * sub - done
        if drop:
            a, m, done = a[drop:], m[drop:], done + drop
        height = TILE - done
        da = dm = None
        for k in range(b):
            col = jnp.broadcast_to(a[:, j0 + k : j0 + k + 1], (height, TILE))
            if done < j0 + b:
                col = jnp.where(line[:height] >= j0 + b - done, col, 0.0)
            ta = col * jnp.broadcast_to(va[k][0:1], (height, TILE))
            tm = col * jnp.broadcast_to(vm[k][0:1], (height, TILE))
            da, dm = (ta, tm) if k == 0 else (da + ta, dm + tm)
        a, m = a - da, m - dm


def split(x):
    high = x.astype(jnp.bfloat16)
    return high, (x - high.astype(jnp.float32)).astype(jnp.bfloat16)


def mul(x, y, transposed=False):
    dims = (((1,), (1 if transposed else 0,)), ((), ()))
    return lax.dot_general(x, y, dims, preferred_element_type=jnp.float32)


def mul3(x, y, transposed=False):
    xh, xl = split(x)
    yh, yl = split(y)
    return mul(xh, yh, transposed) + (mul(xh, yl, transposed) + mul(xl, yh, transposed))


def factor_leading(lead, work, inverse, lower, block_inv, inv_high, inv_low, between):
    width = WIDTH
    work[...] = lead[...].astype(jnp.float32)
    row_of = lax.broadcasted_iota(jnp.int32, (width, width), 0)
    col_of = lax.broadcasted_iota(jnp.int32, (width, width), 1)
    inverse[...] = jnp.where(row_of == col_of, 1.0, 0.0).astype(jnp.float32)

    def store_rows(j0, x):
        for k in range(len(x)):
            block_inv[j0 + k : j0 + k + 1, :] = x[k][0:1, :]

    def step(kb, _):
        between(kb, False)
        o = pl.multiple_of(kb * TILE, TILE)
        here = pl.ds(o, TILE)
        invert_block(work[here, here], store_rows)
        between(kb, True)
        d_inv = block_inv[...]
        below = mul3(work[:, here], d_inv, True)
        line = lax.broadcasted_iota(jnp.int32, (width, TILE), 0)
        lane = lax.broadcasted_iota(jnp.int32, (width, TILE), 1)
        lower[:, here] = jnp.where(line >= lane + o, below, 0.0)
        below = jnp.where(line >= o + TILE, below, 0.0)
        x_rows = mul3(d_inv, inverse[here, :])
        inverse[here, :] = x_rows
        work[...] = work[...] - mul3(below, below, True)
        inverse[...] = inverse[...] - mul3(below, x_rows)
        return 0

    lax.fori_loop(0, PANEL, step, 0)
    high, low = split(inverse[...])
    inv_high[...] = high
    inv_low[...] = low


def update_kernel(inv_high, inv_low, lower, top, panel, front, out, right_high, right_low):
    row_id = lax.axis_index("row")
    block_id = lax.axis_index("sub") * lax.axis_size("col") + lax.axis_index("col")
    tops = top[...]
    high, low = split(mul(inv_high[...], tops) + mul(inv_low[...], tops))
    right_high[...] = high
    right_low[...] = low
    chunk = 256

    @pl.loop(0, panel.shape[0] // chunk)
    def _(t):
        rows = pl.ds(pl.multiple_of(t * chunk, chunk), chunk)
        a_rows = panel[rows, :]
        f_rows = mul(a_rows, inv_high[...], True) + mul(a_rows, inv_low[...], True)
        head = (row_id == 0) & (t < WIDTH // chunk)

        @pl.when(block_id == 0)
        def _():
            out[rows, :] = f_rows

            @pl.when(head)
            def _():
                out[rows, :] = lower[rows, :]

        @pl.when(block_id != 0)
        def _():
            @pl.when(head)
            def _():
                out[rows, :] = front[rows, :]

            @pl.when(jnp.logical_not(head))
            def _():
                fh, fl = split(f_rows)
                out[rows, :] = front[rows, :] - (
                    mul(fh, right_high[...])
                    + (mul(fh, right_low[...]) + mul(fl, right_high[...]))
                )


def apply_update(inv_high, inv_low, lower, top, panel, front):
    vmem = pl.BlockSpec(memory_space=pltpu.VMEM)
    return pl.pallas_call(
        update_kernel,
        out_shape=jax.ShapeDtypeStruct(front.shape, jnp.float32),
        in_specs=[vmem] * 6,
        out_specs=vmem,
        scratch_shapes=[pltpu.VMEM((WIDTH, WIDTH), jnp.bfloat16)] * 2,
        name="apply_update",
    )(inv_high, inv_low, lower, top, panel, front)


def body(child_update, parent_front, tile_map):
    tile_len = TILE
    panel_tiles = PANEL
    sub_count = lax.axis_size("sub")
    row_count = lax.axis_size("row")
    col_count = lax.axis_size("col")
    sub_id = lax.axis_index("sub")
    row_id = lax.axis_index("row")
    col_id = lax.axis_index("col")
    child_rows = child_update.shape[0] // tile_len
    child_cols = child_update.shape[1] // tile_len
    front_rows = parent_front.shape[0] // tile_len
    own_map = lax.dynamic_index_in_dim(tile_map, sub_id, 0, keepdims=False)
    own_cols = lax.dynamic_index_in_dim(
        own_map.reshape(child_cols, col_count), col_id, 1, keepdims=False
    )
    live_cols = own_cols >= 0
    destination = jnp.floor_divide(jnp.floor_divide(own_cols, panel_tiles), col_count)
    slot_index = jnp.remainder(own_cols, panel_tiles)
    dest_hit = destination[None, :] == jnp.arange(sub_count, dtype=jnp.int32)[:, None]
    slot_hit = slot_index[None, :] == jnp.arange(panel_tiles, dtype=jnp.int32)[:, None]
    select = (live_cols[None, None, :] & dest_hit[:, None, :] & slot_hit[None, :, :]).astype(
        jnp.bfloat16
    )
    column_slabs = child_update.reshape(child_rows * tile_len, child_cols, tile_len)
    payload = jnp.einsum(
        "dqk,rky->dqry", select, column_slabs, preferred_element_type=jnp.float32
    ).astype(jnp.bfloat16)
    maps_rows = lax.dynamic_index_in_dim(
        tile_map.reshape(sub_count, child_rows, row_count), row_id, 2, keepdims=False
    )
    local_row = jnp.floor_divide(
        jnp.floor_divide(maps_rows, panel_tiles), row_count
    ) * panel_tiles + jnp.remainder(maps_rows, panel_tiles)
    row_hit = (maps_rows[:, :, None] >= 0) & (
        local_row[:, :, None] == jnp.arange(front_rows, dtype=jnp.int32)[None, None, :]
    )
    place_row = row_hit.astype(jnp.bfloat16)
    arrived = lax.all_to_all(payload, "sub", split_axis=0, concat_axis=0, tiled=True)
    slot_count = arrived.shape[1]
    grid = arrived.reshape(sub_count, slot_count, child_rows, tile_len, tile_len)
    spread = jnp.einsum("ska,sqkyx->ayqx", place_row, grid, preferred_element_type=jnp.float32)
    placed = spread.reshape(front_rows * tile_len, slot_count * tile_len)
    front_local = parent_front.astype(jnp.float32) + placed
    panel, top, inv_high, inv_low, lower = spread_panels(
        front_local.astype(jnp.bfloat16), sub_count, row_count, col_count
    )
    return apply_update(inv_high, inv_low, lower, top, panel, front_local)


def solution(mesh):
    in_specs = (P(("sub", "row"), "col"), P("row", ("sub", "col")), P())
    out_specs = P("row", ("sub", "col"))
    return jax.shard_map(body, mesh=mesh, in_specs=in_specs, out_specs=out_specs, check_vma=False)
```
